32 devices in a mesh: dom: 8 (over z, x), sub: 4 (over y, core).
Axes of the slice: x: 2, y: 2, z: 4, core: 2. Of those that a mesh axis runs over, the one named last changes fastest.
Arguments:
- rhs: float32 [8192, 832], P(('dom', 'sub')), may hold values from -6 to 6
- elem_block: bfloat16 [8192, 64, 64], P(('dom', 'sub')), may hold values from -0.5 to 2.5
- block_inv: bfloat16 [8192, 64, 64], P(('dom', 'sub')), may hold values from -0.2 to 0.8
- flux_jac: float32 [13, 13], replicated, may hold values from -1.75 to 1.75
- face_src: int32 [8192, 6], P(('dom', 'sub')), may hold values from 0 to 2175
- send_face: int32 [160, 128], P(('dom', 'sub')), may hold values from 0 to 1535
- elem_route: int32 [8192], P(('dom', 'sub')), may hold values from 0 to 63
- agg_local: int32 [1024, 2], P(('dom', 'sub')), may hold values from 0 to 63
- coarse_block: float32 [2048, 4, 4], P(('dom', 'sub')), may hold values from -0.5 to 1.3
- coarse_inv: float32 [2048, 4, 4], P(('dom', 'sub')), may hold values from -1 to 4
Outputs:
- adjoint: float32 [8192, 832], P(('dom', 'sub'))
The draws below stay inside these ranges and needn't reach their ends.
Inputs may be any that keep to these rules, and one draw needn't show every extreme that they name: `elem_route`: any owner may receive any slot from any device.
All inputs are finite; a program needn't handle non-finite values.
Results may differ from the reference program's by a relative error of at most 0.0081.
Values sent between devices are 32-bit elements; how exact they have to be, the bound alone decides.
A program may use at most 128 MiB of HBM per device.

```python
import math
import jax
import jax.numpy as jnp
import numpy as np
from jax import lax

COMPS = 13
NODES = 64
FACES = 6
FACE_NODES = 16
MODES = 4
ROUNDS = 5
MOST = 2
ELEM_DEV = 256
SLOTS = 128
AGG_DEV = 64
ELEMS = 8192
AGGS = 2048
DEVICES = 32


def blocked(key, count, width, diag_lo, diag_hi, spread, bound):
    key_diag = jax.random.fold_in(key, 11)
    key_off = jax.random.fold_in(key, 12)
    diagonal = jax.random.uniform(key_diag, (count, width), jnp.float32, diag_lo, diag_hi)
    off = jax.random.normal(key_off, (count, width, width), jnp.float32) * spread
    off = jnp.clip(off, -bound, bound)
    eye = jnp.eye(width, dtype=jnp.float32)
    return off * (1.0 - eye) + eye * diagonal[:, :, None]


def draw_elem_block(key, part):
    return blocked(key, ELEMS, NODES, 1.0, 2.0, 0.1, 0.5).astype(jnp.bfloat16)


def draw_block_inv(key, part):
    return blocked(key, ELEMS, NODES, 0.3, 0.6, 0.04, 0.19).astype(jnp.bfloat16)


def draw_coarse_block(key, part):
    return blocked(key, AGGS, MODES, 0.4, 0.8, 0.1, 0.5)


def draw_coarse_inv(key, part):
    return blocked(key, AGGS, MODES, 1.5, 3.0, 0.2, 1.0)


def set_ends(entries, own_key, low, top_value):
    shape = entries.shape
    place = [jax.random.randint(jax.random.fold_in(own_key, axis), (), 0, shape[axis]) for axis in range(len(shape))]
    entries = entries.at[tuple(place)].set(low)
    longest = shape.index(max(shape))
    place[longest] = (place[longest] + 1) % shape[longest]
    return entries.at[tuple(place)].set(top_value)


def levels(own_key, extent, shards, least, top_value):
    def one(dim, blocks):
        steps = jax.random.uniform(jax.random.fold_in(jax.random.fold_in(own_key, 6), dim), (blocks,), jnp.float32, least / len(shards), top_value / len(shards))
        return jnp.repeat(jnp.exp(steps), extent[dim] // blocks).reshape((-1,) + (1,) * (len(extent) - dim - 1))

    gain = one(*shards[0])
    for cut in shards[1:]:
        gain = gain * one(*cut)
    return gain


def scatter_about(own_key, dims, deviation, most, cuts=(), held_as=jnp.bfloat16):
    values = jax.random.normal(own_key, dims, jnp.float32) * deviation
    if len(cuts) > 0:
        values = levels(own_key, dims, cuts, -0.22, 0.18) * values
    return jnp.clip(values, min=-most, max=most).astype(held_as)


def setup_inputs(seed: int = 0) -> dict:
    streams_of = jax.random.split(jax.random.key(seed), 11)
    rhs = scatter_about(streams_of[0], (ELEMS, COMPS * NODES), 1.0, 6.0, ((0, 32),), jnp.float32)
    elem_block = draw_elem_block(jax.random.fold_in(streams_of[10], 71), 0)
    block_inv = draw_block_inv(jax.random.fold_in(streams_of[10], 71), 0)
    flux_jac = scatter_about(streams_of[3], (COMPS, COMPS), COMPS ** -0.5, 1.75, (), jnp.float32)
    face_src = set_ends(jax.random.randint(streams_of[4], (ELEMS, FACES), 0, FACES * ELEM_DEV + ROUNDS * SLOTS), jax.random.fold_in(streams_of[4], 1), 0, (FACES * ELEM_DEV + ROUNDS * SLOTS) - 1).astype(jnp.int32)
    send_face = set_ends(jax.random.randint(streams_of[5], (DEVICES * ROUNDS, SLOTS), 0, FACES * ELEM_DEV), jax.random.fold_in(streams_of[5], 1), 0, (FACES * ELEM_DEV) - 1).astype(jnp.int32)
    elem_route = set_ends(jax.random.randint(streams_of[6], (ELEMS,), 0, DEVICES * MOST), jax.random.fold_in(streams_of[6], 1), 0, (DEVICES * MOST) - 1).astype(jnp.int32)
    agg_local = set_ends(jax.random.randint(streams_of[7], (DEVICES * DEVICES, MOST), 0, AGG_DEV), jax.random.fold_in(streams_of[7], 1), 0, AGG_DEV - 1).astype(jnp.int32)
    coarse_block = draw_coarse_block(jax.random.fold_in(streams_of[10], 71), 0)
    coarse_inv = draw_coarse_inv(jax.random.fold_in(streams_of[10], 71), 0)
    return {"rhs": rhs, "elem_block": elem_block, "block_inv": block_inv, "flux_jac": flux_jac, "face_src": face_src, "send_face": send_face, "elem_route": elem_route, "agg_local": agg_local, "coarse_block": coarse_block, "coarse_inv": coarse_inv}


HIGHEST = lax.Precision.HIGHEST
PENALTY = 0.5

def node_tables():
    points = np.array([-1.0, -1.0 / math.sqrt(5.0), 1.0 / math.sqrt(5.0), 1.0])
    weights = np.array([1.0, 5.0, 5.0, 1.0]) / 6.0
    grid_i, grid_j, grid_k = np.meshgrid(points, points, points, indexing='ij')
    weight_grid = weights[:, None, None] * weights[None, :, None] * weights[None, None, :] / 8.0
    basis = np.stack([np.ones(64), grid_i.reshape(-1), grid_j.reshape(-1), grid_k.reshape(-1)])
    restrict = basis * weight_grid.reshape(-1)[None, :]
    number = np.arange(64).reshape(4, 4, 4)
    sides = [number[0], number[3], number[:, 0], number[:, 3], number[:, :, 0], number[:, :, 3]]
    face_index = np.stack([side.reshape(-1) for side in sides])
    lift = np.eye(64)[face_index]
    return (basis, restrict, face_index, lift)

def block_apply(pair):
    blocks, field = pair
    rounded = field.astype(jnp.bfloat16).astype(jnp.float32)
    return jnp.einsum('enk,eck->ecn', blocks.astype(jnp.float32), rounded, precision=HIGHEST)

def operate(field, blocks_r, flux_jac, face_rows, send_r, face_index, lift):
    volume = lax.map(block_apply, (blocks_r, field))
    trace = field[:, :, :, face_index.reshape(-1)]
    trace = trace.reshape(DEVICES, ELEM_DEV, COMPS, FACES, FACE_NODES)
    trace = trace.transpose(0, 1, 3, 2, 4).reshape(DEVICES, ELEM_DEV * FACES, COMPS * FACE_NODES)
    received = []
    for round_no in range(ROUNDS):
        partner = jnp.bitwise_xor(jnp.arange(DEVICES, dtype=jnp.int32), jnp.int32(1 << round_no))
        picked = send_r[partner, round_no]
        received.append(trace[partner[:, None], picked])
    table = jnp.concatenate([trace] + received, axis=1)
    beside = jnp.take_along_axis(table, face_rows[:, :, None], axis=1)
    jump = (trace - beside).reshape(DEVICES, ELEM_DEV, FACES, COMPS, FACE_NODES)
    flux = PENALTY * jnp.einsum('defaq,ac->defcq', jump, flux_jac, precision=HIGHEST)
    lifted = jnp.einsum('defcq,fqn->decn', flux, jnp.asarray(lift, jnp.float32), precision=HIGHEST)
    return volume + lifted

def coarse_solve(coarse_rhs, blocks, inverse):
    first = jnp.einsum('amk,ack->acm', inverse, coarse_rhs, precision=HIGHEST)
    left = coarse_rhs - jnp.einsum('amk,ack->acm', blocks, first, precision=HIGHEST)
    return first + jnp.einsum('amk,ack->acm', inverse, left, precision=HIGHEST)

def reference(rhs, elem_block, block_inv, flux_jac, face_src, send_face, elem_route, agg_local, coarse_block, coarse_inv):
    basis, restrict, face_index, lift = node_tables()
    blocks_r = elem_block.reshape(DEVICES, ELEM_DEV, NODES, NODES)
    inverse_r = block_inv.reshape(DEVICES, ELEM_DEV, NODES, NODES)
    source = rhs.reshape(DEVICES, ELEM_DEV, COMPS, NODES)
    face_rows = face_src.reshape(DEVICES, ELEM_DEV * FACES)
    send_r = send_face.reshape(DEVICES, ROUNDS, SLOTS)

    def apply_op(field):
        return operate(field, blocks_r, flux_jac, face_rows, send_r, face_index, lift)

    def sweep(state):
        return state + lax.map(block_apply, (inverse_r, source - apply_op(state)))
    first = lax.map(block_apply, (inverse_r, source))
    second = sweep(first)
    resid = source - apply_op(second)
    partial_value = jnp.einsum('decn,mn->decm', resid, jnp.asarray(restrict, jnp.float32), precision=HIGHEST)
    partial_value = partial_value.reshape(ELEMS, COMPS * MODES)
    owner = elem_route // MOST
    slot = elem_route % MOST
    home = jnp.arange(ELEMS, dtype=jnp.int32) // ELEM_DEV
    agg_r = agg_local.reshape(DEVICES, DEVICES, MOST)
    global_id = (owner * AGG_DEV + agg_r[owner, home, slot]).astype(jnp.int32)
    coarse_rhs = jax.ops.segment_sum(partial_value, global_id, AGGS).reshape(AGGS, COMPS, MODES)
    coarse = coarse_solve(coarse_rhs, coarse_block, coarse_inv).reshape(AGGS, COMPS * MODES)
    correction = coarse[global_id].reshape(DEVICES, ELEM_DEV, COMPS, MODES)
    third = second + jnp.einsum('decm,mn->decn', correction, jnp.asarray(basis, jnp.float32), precision=HIGHEST)
    fourth = sweep(third)
    fifth = sweep(fourth)
    return fifth.reshape(ELEMS, COMPS * NODES)
```

```python
import functools
import math

import jax
import jax.numpy as jnp
import numpy as np
from jax import lax
from jax.experimental import pallas as pl
from jax.experimental.pallas import tpu as pltpu
from jax.sharding import PartitionSpec as P

COMPS = 13
NODES = 64
FACES = 6
FACE_NODES = 16
MODES = 4
ROUNDS = 5
MOST = 2
FLAT = COMPS * NODES
ROW_PITCH = 40
PACK_PITCH = 136
SIDE = COMPS * FACE_NODES
TRACE = FACES * SIDE

HIGHEST = lax.Precision.HIGHEST
PENALTY = 0.5
MESH = pl.DeviceIdType.MESH


def node_tables():
    points = np.array([-1.0, -1.0 / math.sqrt(5.0), 1.0 / math.sqrt(5.0), 1.0])
    weights = np.array([1.0, 5.0, 5.0, 1.0]) / 6.0
    grid_i, grid_j, grid_k = np.meshgrid(points, points, points, indexing="ij")
    weight_grid = weights[:, None, None] * weights[None, :, None] * weights[None, None, :] / 8.0
    basis = np.stack([np.ones(64), grid_i.reshape(-1), grid_j.reshape(-1), grid_k.reshape(-1)])
    restrict = basis * weight_grid.reshape(-1)[None, :]
    number = np.arange(64).reshape(4, 4, 4)
    sides = [number[0], number[3], number[:, 0], number[:, 3], number[:, :, 0], number[:, :, 3]]
    face_index = np.stack([side.reshape(-1) for side in sides])
    return basis, restrict, face_index


def const_tables():
    basis, restrict, face_index = node_tables()
    eye = np.eye(COMPS)
    row_comp = np.tile(np.repeat(eye, FACE_NODES, axis=0), (FACES, 1))
    row_comp = np.pad(row_comp, ((0, 0), (0, 3)))
    col_comp = np.pad(np.repeat(eye, NODES, axis=0), ((0, 0), (0, 3)))
    node = np.eye(NODES)[face_index]
    row_node = np.broadcast_to(node[:, None], (FACES, COMPS, FACE_NODES, NODES)).reshape(TRACE, NODES)
    col_node = np.tile(np.eye(NODES), (COMPS, 1))
    restrict_t = np.zeros((128, FLAT))
    restrict_t[: COMPS * MODES] = np.kron(eye, restrict)
    basis_t = np.zeros((FLAT, 128))
    basis_t[:, : COMPS * MODES] = np.kron(eye, basis.T)
    pick = np.zeros((128, MODES * 128))
    coef = np.zeros((16, MODES * 128))
    for k in range(MODES):
        for c in range(COMPS):
            for m in range(MODES):
                pick[c * MODES + k, k * 128 + c * MODES + m] = 1.0
                coef[m * MODES + k, k * 128 + c * MODES + m] = 1.0
    half = jnp.bfloat16
    return (
        jnp.asarray(row_comp, half),
        jnp.asarray(row_node, half),
        jnp.asarray(col_comp.T, half),
        jnp.asarray(col_node.T, half),
        jnp.asarray(col_comp, half),
        jnp.asarray(col_node, half),
        jnp.asarray(row_comp.T, half),
        jnp.asarray(row_node.T, half),
        jnp.asarray(restrict_t, jnp.float32),
        jnp.asarray(basis_t, jnp.float32),
        jnp.asarray(pick, jnp.float32),
        jnp.asarray(coef, jnp.float32),
    )


def dot(a, b):
    return jnp.dot(a, b, preferred_element_type=jnp.float32)


def dot_exact(a, b, dims=((1,), (0,))):
    return lax.dot_general(
        a, b, (dims, ((), ())), precision=HIGHEST, preferred_element_type=jnp.float32
    )


def kernel(
    count, subs,
    rhs, blocks, inverse, jac, face_src, send_face, route, agg_local, cblock, cinv,
    row_comp, row_node, comp_col, node_col, col_comp, col_node, comp_row, node_row,
    restrict_t, basis_t, pick, coef,
    out,
    stage, block_w, inverse_w, rhs_lam, state, work, flux_lam, delta, lift_t, trace_t, pick_local, pick_remote, pick_send,
    half_field, lifted, trace, beside, table, jump, sending, arriving,
    bucket, incoming, reply, answer, jac_pad, flat_block, flat_inv,
    send_sem, recv_sem, give_sem, take_sem, back_sem, home_sem,
):
    elements = rhs.shape[1]
    tiles = elements // 128
    own = FACES * elements
    far = ROUNDS * 128
    me = lax.axis_index("dom") * subs + lax.axis_index("sub")

    def place(flat):
        return (flat // subs, flat % subs)

    def partner(k):
        bit = 1 << k
        return me + bit * (1 - 2 * ((me // bit) % 2))

    barrier = pltpu.get_barrier_semaphore()

    def greet(step, carry):
        pl.semaphore_signal(
            barrier, inc=1, device_id=place((me + step) % count), device_id_type=MESH
        )
        return carry

    lax.fori_loop(1, count, greet, 0)

    half_lanes = lax.broadcasted_iota(jnp.int32, (32, 128), 1) < NODES
    pairs = elements // 8

    def pack(source, target):
        def transpose(n, carry):
            rows = source[n].astype(jnp.float32)
            flat = jnp.concatenate([rows[:, :128], rows[:, 128:]], axis=0).T
            for y in range(2):
                even, odd = flat[y * 64 : y * 64 + 32], flat[y * 64 + 32 : y * 64 + 64]
                stage[y, pl.ds(n, pairs, stride=PACK_PITCH), :] = jnp.where(half_lanes, even, odd)
                stage[y, pl.ds(NODES + n, pairs, stride=PACK_PITCH), :] = jnp.where(half_lanes, odd, even)
            return carry

        lax.fori_loop(0, NODES, transpose, 0, unroll=8)

        def cast(j, carry):
            rows = pl.ds(pl.multiple_of(j * PACK_PITCH, 8), 128)
            for y in range(2):
                target[y, j] = stage[y, rows, :].astype(jnp.bfloat16)
            return carry

        lax.fori_loop(0, pairs, cast, 0, unroll=4)

    lane = lax.broadcasted_iota(jnp.int32, (NODES, 128), 1)
    odd_lane = (lane // 32) % 2 == 1

    def to_lam(source, target):
        for c in range(COMPS):
            rows = slice(c * NODES, (c + 1) * NODES)
            low, high = source[rows, :128], source[rows, 128:]
            flat = jnp.concatenate(
                [jnp.where(odd_lane, high, low), jnp.where(odd_lane, low, high)], axis=0
            ).T
            for y in range(2):
                for x in range(2):
                    start = y * 64 + x * 32
                    target[y, pl.ds(16 * x + c, pairs, stride=ROW_PITCH), :] = flat[start : start + 32]

    def from_lam(source, emit):
        for c in range(COMPS):
            flat = jnp.concatenate(
                [
                    source[y, pl.ds(16 * x + c, pairs, stride=ROW_PITCH), :]
                    for y in range(2)
                    for x in range(2)
                ],
                axis=0,
            ).T
            even, odd = flat[:NODES], flat[NODES:]
            rows = slice(c * NODES, (c + 1) * NODES)
            emit(rows, slice(0, 128), jnp.where(odd_lane, odd, even))
            emit(rows, slice(128, 256), jnp.where(odd_lane, even, odd))

    low_half = half_lanes[:16]
    blank = jnp.zeros((16, 128), jnp.float32)

    def apply_blocks(load, weights, emit):
        def body(g, carry):
            for y in range(2):
                parts = []
                for i in range(2):
                    row = pl.multiple_of((2 * g + i) * ROW_PITCH, 8)
                    even = load(y, pl.ds(row, 16))
                    odd = pltpu.roll(load(y, pl.ds(row + 16, 16)), NODES, 1)
                    parts += [
                        jnp.where(low_half, even, blank),
                        jnp.where(low_half, odd, blank),
                        jnp.where(low_half, blank, even),
                        jnp.where(low_half, blank, odd),
                    ]
                left = jnp.concatenate(parts, axis=0).astype(jnp.bfloat16)
                right = weights[y, pl.ds(2 * g, 2)].reshape(256, 128)
                both = lax.dot_general(
                    left, right, (((1,), (1,)), ((), ())), preferred_element_type=jnp.float32
                )
                for i in range(2):
                    row = pl.multiple_of((2 * g + i) * ROW_PITCH, 8)
                    value = both[64 * i : 64 * i + 64, 128 * i : 128 * i + 128]
                    emit(y, pl.ds(row, 16), jnp.where(low_half, value[:16], value[32:48]))
                    emit(y, pl.ds(row + 16, 16), jnp.where(low_half, value[48:], value[16:32]))
            return carry

        lax.fori_loop(0, pairs // 2, body, 0, unroll=8)

    def load_from(source):
        return lambda y, rows: source[y, rows, :]

    def store(target):
        def emit(y, rows, value):
            target[y, rows, :] = value
        return emit

    def add_to(target):
        def emit(y, rows, value):
            target[y, rows, :] = target[y, rows, :] + value
        return emit

    pack(inverse, inverse_w)
    to_lam(rhs, rhs_lam)
    apply_blocks(load_from(rhs_lam), inverse_w, store(state))
    pack(blocks, block_w)

    jac_pad[...] = jnp.zeros_like(jac_pad)
    jac_pad[:COMPS, :COMPS] = jac[...]
    spread_jac = lax.dot_general(
        jac_pad[...].astype(jnp.bfloat16),
        comp_col[...],
        (((0,), (0,)), ((), ())),
        preferred_element_type=jnp.float32,
    )[:16].astype(jnp.bfloat16)
    for m in range(MODES):
        flat_block[m * MODES : (m + 1) * MODES, :] = cblock[m]
        flat_inv[m * MODES : (m + 1) * MODES, :] = cinv[m]
    inv_wide = dot_exact(flat_inv[...], coef[...], ((0,), (0,)))
    block_wide = dot_exact(flat_block[...], coef[...], ((0,), (0,)))

    def tables(f, carry):
        rows = pl.ds(pl.multiple_of(f * SIDE, SIDE), SIDE)
        value = dot(row_comp[rows, :], spread_jac) * dot(row_node[rows, :], node_col[...])
        trace_t[rows, :] = (PENALTY * value).astype(jnp.bfloat16)
        return carry

    lax.fori_loop(0, FACES, tables, 0)

    def lifts(i, carry):
        rows = pl.ds(pl.multiple_of(i * 208, 208), 208)
        value = dot(col_comp[rows, :], comp_row[...]) * dot(col_node[rows, :], node_row[...])
        lift_t[rows, :] = value.astype(jnp.bfloat16)
        return carry

    lax.fori_loop(0, FLAT // 208, lifts, 0)

    def column(row):
        element = (row * 43691) >> 18
        return jnp.where(row < own, (row - element * FACES) * elements + element, row)

    def one_hot(rows, wanted):
        index = lax.broadcasted_iota(jnp.int32, (rows, wanted.shape[1]), 0)
        return jnp.where(index == wanted, 1.0, 0.0).astype(jnp.bfloat16)

    for k in range(ROUNDS):
        pick_send[:, k * 128 : (k + 1) * 128] = one_hot(own, column(send_face[k : k + 1, :]))
    for f in range(FACES):
        wanted = column(face_src[f : f + 1, :])
        pick_local[f] = one_hot(own, wanted)
        pick_remote[f] = one_hot(far, wanted - own)
    route_row = (route[...] // MOST) * 8 + route[...] % MOST
    to_bucket = (
        lax.broadcasted_iota(jnp.int32, (count * 8, elements), 0) == route_row
    ).astype(jnp.float32)

    pl.semaphore_wait(barrier, count - 1)

    def operate(number):
        def emit_half(rows, lanes, value):
            half_field[rows, lanes] = value.astype(jnp.bfloat16)

        from_lam(state, emit_half)

        def traces(third, carry):
            rows = pl.ds(pl.multiple_of(third * 2 * SIDE, 2 * SIDE), 2 * SIDE)
            value = dot(trace_t[rows, :], half_field[...])
            trace[rows, :] = value
            column_pair = pl.ds(pl.multiple_of(third * 2 * elements, 128), elements)
            table[:, column_pair] = value[:SIDE].astype(jnp.bfloat16)
            column_pair = pl.ds(pl.multiple_of((third * 2 + 1) * elements, 128), elements)
            table[:, column_pair] = value[SIDE:].astype(jnp.bfloat16)
            return carry

        lax.fori_loop(0, FACES // 2, traces, 0)
        outgoing = dot(table[:, :own], pick_send[...])
        copies = []
        for k in range(ROUNDS):
            sending[k] = outgoing[:, k * 128 : (k + 1) * 128]
            copy = pltpu.make_async_remote_copy(
                src_ref=sending.at[k],
                dst_ref=arriving.at[number, k],
                send_sem=send_sem.at[number, k],
                recv_sem=recv_sem.at[number, k],
                device_id=place(partner(k)),
                device_id_type=MESH,
            )
            copy.start()
            copies.append(copy)
        apply_blocks(load_from(state), block_w, store(work))

        def near(f, carry):
            rows = pl.ds(pl.multiple_of(f * SIDE, SIDE), SIDE)
            beside[rows, :] = trace[rows, :] - dot(table[:, :own], pick_local[f])
            return carry

        lax.fori_loop(0, FACES, near, 0)
        for k in range(ROUNDS):
            copies[k].wait()
            table[:, own + k * 128 : own + (k + 1) * 128] = arriving[number, k].astype(
                jnp.bfloat16
            )

        def beyond(f, carry):
            rows = pl.ds(pl.multiple_of(f * SIDE, SIDE), SIDE)
            value = beside[rows, :] - dot(table[:, own:], pick_remote[f])
            jump[rows, :] = value.astype(jnp.bfloat16)
            return carry

        lax.fori_loop(0, FACES, beyond, 0)

        def lift(i, carry):
            rows = pl.ds(pl.multiple_of(i * 416, 416), 416)
            lifted[rows, :] = dot(lift_t[rows, :], jump[...])
            return carry

        lax.fori_loop(0, FLAT // 416, lift, 0)

    def residual(y, rows):
        return rhs_lam[y, rows, :] - work[y, rows, :] - flux_lam[y, rows, :]

    def sweep(number):
        operate(number)
        to_lam(lifted, flux_lam)
        apply_blocks(residual, inverse_w, add_to(state))

    def exchange(source, target, sent, got):
        def copy_of(step):
            other = (me + step) % count
            return pltpu.make_async_remote_copy(
                src_ref=source.at[other],
                dst_ref=target.at[me],
                send_sem=sent.at[step],
                recv_sem=got.at[step],
                device_id=place(other),
                device_id_type=MESH,
            )

        def begin(step, carry):
            copy_of(step).start()
            return carry

        def finish(step, carry):
            copy_of(step).wait()
            return carry

        lax.fori_loop(1, count, begin, 0)
        target[me] = source[me]
        lax.fori_loop(1, count, finish, 0)

    sweep(0)
    operate(1)
    def emit_residual(rows, lanes, value):
        lifted[rows, lanes] = rhs[rows, lanes] - lifted[rows, lanes] - value

    from_lam(work, emit_residual)
    partial = dot_exact(restrict_t[...], lifted[...])
    bucket[...] = dot_exact(to_bucket, partial, ((1,), (1,))).reshape(count, 8, 128)
    exchange(bucket, incoming, give_sem, take_sem)
    owned = cblock.shape[2]
    members = [
        (
            lax.broadcasted_iota(jnp.int32, (owned, count), 0) == agg_local[s : s + 1, :]
        ).astype(jnp.float32)
        for s in range(MOST)
    ]
    coarse_rhs = sum(dot_exact(members[s], incoming[:, s, :]) for s in range(MOST))

    def modal(wide, value):
        product = wide * dot_exact(value, pick[...])
        return (
            product[:, :128] + product[:, 128:256] + product[:, 256:384] + product[:, 384:]
        )

    first = modal(inv_wide, coarse_rhs)
    solved = first + modal(inv_wide, coarse_rhs - modal(block_wide, first))
    reply[...] = jnp.zeros_like(reply)
    for s in range(MOST):
        reply[:, s, :] = dot_exact(members[s], solved, ((0,), (0,)))
    exchange(reply, answer, back_sem, home_sem)
    correction = dot_exact(answer[...].reshape(count * 8, 128), to_bucket, ((0,), (0,)))
    lifted[...] = dot_exact(basis_t[...], correction)
    to_lam(lifted, delta)
    state[...] = state[...] + delta[...]

    def last_sweeps(number, carry):
        sweep(number)
        return carry

    lax.fori_loop(2, 4, last_sweeps, 0)

    def emit_out(rows, lanes, value):
        out[rows, lanes] = value

    from_lam(state, emit_out)


def local(
    rhs,
    elem_block,
    block_inv,
    flux_jac,
    face_src,
    send_face,
    elem_route,
    agg_local,
    coarse_block,
    coarse_inv,
):
    elements = rhs.shape[0]
    count = lax.axis_size(("dom", "sub"))
    subs = lax.axis_size("sub")
    owned = coarse_block.shape[0]
    tiles = elements // 128
    pairs = elements // 8
    own = FACES * elements
    far = ROUNDS * 128
    f32, half = jnp.float32, jnp.bfloat16
    dma = pltpu.SemaphoreType.DMA
    result = pl.pallas_call(
        functools.partial(kernel, count, subs),
        out_shape=jax.ShapeDtypeStruct((FLAT, elements), f32),
        in_specs=[pl.BlockSpec(memory_space=pltpu.VMEM)] * 22,
        out_specs=pl.BlockSpec(memory_space=pltpu.VMEM),
        scratch_shapes=[
            pltpu.VMEM((tiles, pairs * PACK_PITCH, 128), f32),
            pltpu.VMEM((tiles, pairs, 128, 128), half),
            pltpu.VMEM((tiles, pairs, 128, 128), half),
            pltpu.VMEM((tiles, pairs * ROW_PITCH, 128), f32),
            pltpu.VMEM((tiles, pairs * ROW_PITCH, 128), f32),
            pltpu.VMEM((tiles, pairs * ROW_PITCH, 128), f32),
            pltpu.VMEM((tiles, pairs * ROW_PITCH, 128), f32),
            pltpu.VMEM((tiles, pairs * ROW_PITCH, 128), f32),
            pltpu.VMEM((FLAT, TRACE), half),
            pltpu.VMEM((TRACE, FLAT), half),
            pltpu.VMEM((FACES, own, elements), half),
            pltpu.VMEM((FACES, far, elements), half),
            pltpu.VMEM((own, far), half),
            pltpu.VMEM((FLAT, elements), half),
            pltpu.VMEM((FLAT, elements), f32),
            pltpu.VMEM((TRACE, elements), f32),
            pltpu.VMEM((TRACE, elements), f32),
            pltpu.VMEM((SIDE, own + far), half),
            pltpu.VMEM((TRACE, elements), half),
            pltpu.VMEM((ROUNDS, SIDE, 128), f32),
            pltpu.VMEM((4, ROUNDS, SIDE, 128), f32),
            pltpu.VMEM((count, 8, 128), f32),
            pltpu.VMEM((count, 8, 128), f32),
            pltpu.VMEM((count, 8, 128), f32),
            pltpu.VMEM((count, 8, 128), f32),
            pltpu.VMEM((16, 128), f32),
            pltpu.VMEM((MODES * MODES, owned), f32),
            pltpu.VMEM((MODES * MODES, owned), f32),
            dma((4, ROUNDS)),
            dma((4, ROUNDS)),
            dma((count,)),
            dma((count,)),
            dma((count,)),
            dma((count,)),
        ],
        compiler_params=pltpu.CompilerParams(
            collective_id=0, has_side_effects=True, vmem_limit_bytes=58 * 2**20
        ),
    )(
        rhs.T,
        elem_block.transpose(1, 2, 0),
        block_inv.transpose(1, 2, 0),
        flux_jac,
        face_src.T,
        send_face,
        elem_route.reshape(1, elements),
        agg_local.T,
        coarse_block.transpose(1, 2, 0),
        coarse_inv.transpose(1, 2, 0),
        *const_tables(),
    )
    return result.T


def solution(mesh):
    return jax.shard_map(
        local,
        mesh=mesh,
        in_specs=(
            P(("dom", "sub"), None),
            P(("dom", "sub"), None, None),
            P(("dom", "sub"), None, None),
            P(),
            P(("dom", "sub"), None),
            P(("dom", "sub"), None),
            P(("dom", "sub")),
            P(("dom", "sub"), None),
            P(("dom", "sub"), None, None),
            P(("dom", "sub"), None, None),
        ),
        out_specs=P(("dom", "sub"), None),
        check_vma=False,
    )
```

```python
import functools
import math

import jax
import jax.numpy as jnp
import numpy as np
from jax import lax
from jax.experimental import pallas as pl
from jax.experimental.pallas import tpu as pltpu
from jax.sharding import PartitionSpec as P

COMPS = 13
NODES = 64
FACES = 6
FACE_NODES = 16
MODES = 4
ROUNDS = 5
MOST = 2
FLAT = COMPS * NODES
ROW_PITCH = 40
PACK_PITCH = 136
SIDE = COMPS * FACE_NODES
TRACE = FACES * SIDE

HIGHEST = lax.Precision.HIGHEST
PENALTY = 0.5
MESH = pl.DeviceIdType.MESH


def node_tables():
    points = np.array([-1.0, -1.0 / math.sqrt(5.0), 1.0 / math.sqrt(5.0), 1.0])
    weights = np.array([1.0, 5.0, 5.0, 1.0]) / 6.0
    grid_i, grid_j, grid_k = np.meshgrid(points, points, points, indexing="ij")
    weight_grid = weights[:, None, None] * weights[None, :, None] * weights[None, None, :] / 8.0
    basis = np.stack([np.ones(64), grid_i.reshape(-1), grid_j.reshape(-1), grid_k.reshape(-1)])
    restrict = basis * weight_grid.reshape(-1)[None, :]
    number = np.arange(64).reshape(4, 4, 4)
    sides = [number[0], number[3], number[:, 0], number[:, 3], number[:, :, 0], number[:, :, 3]]
    face_index = np.stack([side.reshape(-1) for side in sides])
    return basis, restrict, face_index


def const_tables():
    basis, restrict, face_index = node_tables()
    eye = np.eye(COMPS)
    comp_row = np.pad(np.tile(np.repeat(eye, FACE_NODES, axis=0), (FACES, 1)), ((0, 0), (0, 3))).T
    col_comp = np.pad(np.repeat(eye, NODES, axis=0), ((0, 0), (0, 3)))
    node = np.eye(NODES)[face_index]
    row_node = np.broadcast_to(node[:, None], (FACES, COMPS, FACE_NODES, NODES)).reshape(TRACE, NODES)
    col_node = np.tile(np.eye(NODES), (COMPS, 1))
    select = np.kron(np.eye(2), node.reshape(FACES * FACE_NODES, NODES))
    restrict_t = np.zeros((128, FLAT))
    restrict_t[: COMPS * MODES] = np.kron(eye, restrict)
    basis_t = np.zeros((FLAT, 128))
    basis_t[:, : COMPS * MODES] = np.kron(eye, basis.T)
    pick = np.zeros((128, MODES * 128))
    coef = np.zeros((16, MODES * 128))
    for k in range(MODES):
        for c in range(COMPS):
            for m in range(MODES):
                pick[c * MODES + k, k * 128 + c * MODES + m] = 1.0
                coef[m * MODES + k, k * 128 + c * MODES + m] = 1.0
    half = jnp.bfloat16
    return (
        jnp.asarray(comp_row, half),
        jnp.asarray(row_node.T, half),
        jnp.asarray(col_comp, half),
        jnp.asarray(col_node, half),
        jnp.asarray(select, half),
        *parts_of(restrict_t),
        *parts_of(basis_t),
        jnp.asarray(pick, half),
        jnp.asarray(coef, half),
    )


def parts_of(table):
    table = np.asarray(table, np.float32)
    high = table.astype(jnp.bfloat16)
    return jnp.asarray(high), jnp.asarray((table - high.astype(np.float32)).astype(jnp.bfloat16))


def dot(a, b):
    return jnp.dot(a, b, preferred_element_type=jnp.float32)


def general(a, b, dims):
    return lax.dot_general(a, b, (dims, ((), ())), preferred_element_type=jnp.float32)


def split(value):
    high = value.astype(jnp.bfloat16)
    return high, (value - high.astype(jnp.float32)).astype(jnp.bfloat16)


def dot_ones(ones, value, dims=((1,), (0,))):
    high, low = split(value)
    return general(ones, high, dims) + general(ones, low, dims)


def dot_parts(table, value):
    high, low = split(value)
    return dot(table[0], high) + (dot(table[0], low) + dot(table[1], high))


def kernel(
    count, subs,
    rhs, blocks, inverse, jac, face_src, send_face, route, agg_local, cblock, cinv,
    comp_row, node_row, col_comp, col_node, select,
    restrict_high, restrict_low, basis_high, basis_low, pick, coef,
    out,
    stage, block_w, inverse_w, rhs_lam, state, work, flux_lam, delta,
    lift_t, pick_local, pick_remote, pick_send,
    lifted, near, table, landed, jump, sending, arriving,
    bucket, incoming, reply, answer, jac_pad, flat_block, flat_inv,
    send_sem, recv_sem, give_sem, take_sem, back_sem, home_sem,
):
    elements = rhs.shape[1]
    tiles = elements // 128
    own = FACES * elements
    far = ROUNDS * 128
    me = lax.axis_index("dom") * subs + lax.axis_index("sub")

    def place(flat):
        return (flat // subs, flat % subs)

    def partner(k):
        bit = 1 << k
        return me + bit * (1 - 2 * ((me // bit) % 2))

    barrier = pltpu.get_barrier_semaphore()

    def greet(step, carry):
        pl.semaphore_signal(
            barrier, inc=1, device_id=place((me + step) % count), device_id_type=MESH
        )
        return carry

    lax.fori_loop(1, count, greet, 0)

    half_lanes = lax.broadcasted_iota(jnp.int32, (32, 128), 1) < NODES
    pairs = elements // 8

    def pack(source, target):
        def transpose(n, carry):
            rows = source[n].astype(jnp.float32)
            flat = jnp.concatenate([rows[:, :128], rows[:, 128:]], axis=0).T
            for y in range(2):
                even, odd = flat[y * 64 : y * 64 + 32], flat[y * 64 + 32 : y * 64 + 64]
                stage[y, pl.ds(n, pairs, stride=PACK_PITCH), :] = jnp.where(half_lanes, even, odd)
                stage[y, pl.ds(NODES + n, pairs, stride=PACK_PITCH), :] = jnp.where(half_lanes, odd, even)
            return carry

        lax.fori_loop(0, NODES, transpose, 0, unroll=8)

        def cast(j, carry):
            rows = pl.ds(pl.multiple_of(j * PACK_PITCH, 8), 128)
            for y in range(2):
                target[y, j] = stage[y, rows, :].astype(jnp.bfloat16)
            return carry

        lax.fori_loop(0, pairs, cast, 0, unroll=4)

    lane = lax.broadcasted_iota(jnp.int32, (NODES, 128), 1)
    odd_lane = (lane // 32) % 2 == 1

    def to_lam(source, target):
        for c in range(COMPS):
            rows = slice(c * NODES, (c + 1) * NODES)
            low, high = source[rows, :128], source[rows, 128:]
            flat = jnp.concatenate(
                [jnp.where(odd_lane, high, low), jnp.where(odd_lane, low, high)], axis=0
            ).T
            for y in range(2):
                for x in range(2):
                    start = y * 64 + x * 32
                    target[y, pl.ds(16 * x + c, pairs, stride=ROW_PITCH), :] = flat[start : start + 32]

    def from_lam(source, emit):
        for c in range(COMPS):
            flat = jnp.concatenate(
                [
                    source[y, pl.ds(16 * x + c, pairs, stride=ROW_PITCH), :]
                    for y in range(2)
                    for x in range(2)
                ],
                axis=0,
            ).T
            even, odd = flat[:NODES], flat[NODES:]
            rows = slice(c * NODES, (c + 1) * NODES)
            emit(rows, slice(0, 128), jnp.where(odd_lane, odd, even))
            emit(rows, slice(128, 256), jnp.where(odd_lane, even, odd))

    low_half = half_lanes[:16]
    blank = jnp.zeros((16, 128), jnp.float32)

    def apply_blocks(load, weights, emit):
        def body(g, carry):
            for y in range(2):
                parts = []
                for i in range(2):
                    row = pl.multiple_of((2 * g + i) * ROW_PITCH, 8)
                    even = load(y, pl.ds(row, 16))
                    odd = pltpu.roll(load(y, pl.ds(row + 16, 16)), NODES, 1)
                    parts += [
                        jnp.where(low_half, even, blank),
                        jnp.where(low_half, odd, blank),
                        jnp.where(low_half, blank, even),
                        jnp.where(low_half, blank, odd),
                    ]
                left = jnp.concatenate(parts, axis=0).astype(jnp.bfloat16)
                right = weights[y, pl.ds(2 * g, 2)].reshape(256, 128)
                both = lax.dot_general(
                    left, right, (((1,), (1,)), ((), ())), preferred_element_type=jnp.float32
                )
                for i in range(2):
                    row = pl.multiple_of((2 * g + i) * ROW_PITCH, 8)
                    value = both[64 * i : 64 * i + 64, 128 * i : 128 * i + 128]
                    emit(y, pl.ds(row, 16), jnp.where(low_half, value[:16], value[32:48]))
                    emit(y, pl.ds(row + 16, 16), jnp.where(low_half, value[48:], value[16:32]))
            return carry

        lax.fori_loop(0, pairs // 2, body, 0, unroll=8)

    def load_from(source):
        return lambda y, rows: source[y, rows, :]

    def store(target):
        def emit(y, rows, value):
            target[y, rows, :] = value
        return emit

    def add_to(target):
        def emit(y, rows, value):
            target[y, rows, :] = target[y, rows, :] + value
        return emit

    pack(inverse, inverse_w)
    to_lam(rhs, rhs_lam)
    apply_blocks(load_from(rhs_lam), inverse_w, store(state))

    def column(row):
        element = (row * 43691) >> 18
        return jnp.where(row < own, (row - element * FACES) * elements + element, row)

    def one_hot(rows, wanted, value=1.0):
        index = lax.broadcasted_iota(jnp.int32, (rows, wanted.shape[1]), 0)
        return jnp.where(index == wanted, value, 0.0).astype(jnp.bfloat16)

    for k in range(ROUNDS):
        wanted = column(send_face[k : k + 1, :])

        def send_rows(f, carry):
            rows = pl.ds(pl.multiple_of(f * elements, elements), elements)
            pick_send[rows, k * 128 : (k + 1) * 128] = one_hot(elements, wanted - f * elements)
            return carry

        lax.fori_loop(0, FACES, send_rows, 0)

    def local_tables():
        jac_pad[...] = jnp.zeros_like(jac_pad)
        jac_pad[:COMPS, :COMPS] = PENALTY * jac[...]
        spread_jac = general(jac_pad[...].astype(jnp.bfloat16), comp_row[...], ((0,), (0,)))[
            :16
        ].astype(jnp.bfloat16)

        def lifts(i, carry):
            rows = pl.ds(pl.multiple_of(i * 208, 208), 208)
            value = dot(col_comp[rows, :], spread_jac) * dot(col_node[rows, :], node_row[...])
            lift_t[rows, :] = value.astype(jnp.bfloat16)
            return carry

        lax.fori_loop(0, FLAT // 208, lifts, 0)
        row = lax.broadcasted_iota(jnp.int32, (elements, elements), 0)
        mine = jnp.where(row == lax.broadcasted_iota(jnp.int32, (elements, elements), 1), 1.0, 0.0)
        for f in range(FACES):
            lanes = slice(f * elements, (f + 1) * elements)
            wanted = column(face_src[f : f + 1, :])

            def local_rows(g, carry):
                rows = pl.ds(pl.multiple_of(g * elements, elements), elements)
                pick_local[rows, lanes] = one_hot(elements, wanted - g * elements, -1.0)
                return carry

            lax.fori_loop(0, FACES, local_rows, 0)
            pick_local[lanes, lanes] = pick_local[lanes, lanes] + mine.astype(jnp.bfloat16)

            def remote_rows(k, carry):
                rows = pl.ds(pl.multiple_of(k * 128, 128), 128)
                pick_remote[rows, lanes] = one_hot(128, wanted - own - k * 128, -1.0)
                return carry

            lax.fori_loop(0, ROUNDS, remote_rows, 0)

    odd_face = (lax.broadcasted_iota(jnp.int32, (FACES * FACE_NODES, 128), 1) // 32) % 2 == 1

    def traces():
        for c in range(COMPS):
            flat = jnp.concatenate(
                [
                    state[y, pl.ds(16 * x + c, pairs, stride=ROW_PITCH), :]
                    for y in range(2)
                    for x in range(2)
                ],
                axis=0,
            ).astype(jnp.bfloat16)
            value = general(select[...], flat, ((1,), (1,)))
            even, odd = value[: FACES * FACE_NODES], value[FACES * FACE_NODES :]
            low = jnp.where(odd_face, odd, even).astype(jnp.bfloat16)
            high = jnp.where(odd_face, even, odd).astype(jnp.bfloat16)
            rows = slice(c * FACE_NODES, (c + 1) * FACE_NODES)
            for f in range(FACES):
                part = slice(f * FACE_NODES, (f + 1) * FACE_NODES)
                table[rows, f * elements : f * elements + 128] = low[part]
                table[rows, f * elements + 128 : (f + 1) * elements] = high[part]

    def operate(number, between=None):
        traces()
        copies = {}
        for group in ((4, 3), (2, 1, 0)):
            lanes = slice(min(group) * 128, (max(group) + 1) * 128)
            outgoing = dot(table[...], pick_send[:, lanes])
            for k in group:
                start = (k - min(group)) * 128
                sending[k] = outgoing[:, start : start + 128]
                copies[k] = pltpu.make_async_remote_copy(
                    src_ref=sending.at[k],
                    dst_ref=arriving.at[number, k],
                    send_sem=send_sem.at[number, k],
                    recv_sem=recv_sem.at[number, k],
                    device_id=place(partner(k)),
                    device_id_type=MESH,
                )
                copies[k].start()
        if between is not None:
            between()
        near[...] = dot(table[...], pick_local[...])
        apply_blocks(load_from(state), block_w, store(work))

        def land(k):
            copies[k].wait()
            landed[:, k * 128 : (k + 1) * 128] = arriving[number, k].astype(jnp.bfloat16)

        for k in (0, 1, 2):
            land(k)
        near[...] = near[...] + dot(landed[:, : 3 * 128], pick_remote[: 3 * 128, :])
        for k in (3, 4):
            land(k)
        value = near[...] + dot(landed[:, 3 * 128 :], pick_remote[3 * 128 :, :])
        for f in range(FACES):
            jump[f * SIDE : (f + 1) * SIDE, :] = value[:, f * elements : (f + 1) * elements].astype(
                jnp.bfloat16
            )
        lifted[...] = dot(lift_t[...], jump[...])

    def residual(y, rows):
        return rhs_lam[y, rows, :] - work[y, rows, :] - flux_lam[y, rows, :]

    def sweep(number):
        operate(number)
        to_lam(lifted, flux_lam)
        apply_blocks(residual, inverse_w, add_to(state))

    def exchange(source, target, sent, got):
        def copy_of(step):
            other = (me + step) % count
            return pltpu.make_async_remote_copy(
                src_ref=source.at[other, pl.ds(0, MOST)],
                dst_ref=target.at[me, pl.ds(0, MOST)],
                send_sem=sent.at[step],
                recv_sem=got.at[step],
                device_id=place(other),
                device_id_type=MESH,
            )

        def begin(step, carry):
            copy_of(step).start()
            return carry

        def finish(step, carry):
            copy_of(step).wait()
            return carry

        lax.fori_loop(1, count, begin, 0)
        target[me] = source[me]
        lax.fori_loop(1, count, finish, 0)

    def behind_first():
        local_tables()
        pack(blocks, block_w)

    for m in range(MODES):
        flat_block[m * MODES : (m + 1) * MODES, :] = cblock[m]
        flat_inv[m * MODES : (m + 1) * MODES, :] = cinv[m]
    pl.semaphore_wait(barrier, count - 1)
    operate(0, behind_first)
    to_lam(lifted, flux_lam)
    apply_blocks(residual, inverse_w, add_to(state))
    operate(1)

    def emit_residual(rows, lanes, value):
        lifted[rows, lanes] = rhs[rows, lanes] - lifted[rows, lanes] - value

    from_lam(work, emit_residual)
    partial = dot_parts((restrict_high[...], restrict_low[...]), lifted[...])
    route_row = (route[...] // MOST) * 8 + route[...] % MOST
    to_bucket = one_hot(count * 8, route_row)
    bucket[...] = dot_ones(to_bucket, partial, ((1,), (1,))).reshape(count, 8, 128)
    exchange(bucket, incoming, give_sem, take_sem)
    owned = cblock.shape[2]
    members = [one_hot(owned, agg_local[s : s + 1, :]) for s in range(MOST)]
    coarse_rhs = sum(dot_ones(members[s], incoming[:, s, :]) for s in range(MOST))
    inv_high, inv_low = split(flat_inv[...])
    inv_wide = general(inv_high, coef[...], ((0,), (0,))) + general(inv_low, coef[...], ((0,), (0,)))
    block_high, block_low = split(flat_block[...])
    block_wide = general(block_high, coef[...], ((0,), (0,))) + general(
        block_low, coef[...], ((0,), (0,))
    )

    def modal(wide, value):
        high, low = split(value)
        product = wide * (dot(high, pick[...]) + dot(low, pick[...]))
        return (
            product[:, :128] + product[:, 128:256] + product[:, 256:384] + product[:, 384:]
        )

    first = modal(inv_wide, coarse_rhs)
    solved = first + modal(inv_wide, coarse_rhs - modal(block_wide, first))
    reply[...] = jnp.zeros_like(reply)
    for s in range(MOST):
        reply[:, s, :] = dot_ones(members[s], solved, ((0,), (0,)))
    exchange(reply, answer, back_sem, home_sem)
    slot = lax.broadcasted_iota(jnp.int32, (count * 8, 128), 0) % 8
    returned = jnp.where(slot < MOST, answer[...].reshape(count * 8, 128), 0.0)
    high, low = split(returned)
    correction = general(high, to_bucket, ((0,), (0,))) + general(low, to_bucket, ((0,), (0,)))
    lifted[...] = dot_parts((basis_high[...], basis_low[...]), correction)
    to_lam(lifted, delta)
    state[...] = state[...] + delta[...]

    def last_sweeps(number, carry):
        sweep(number)
        return carry

    lax.fori_loop(2, 4, last_sweeps, 0)

    def emit_out(rows, lanes, value):
        out[rows, lanes] = value

    from_lam(state, emit_out)


def local(
    rhs,
    elem_block,
    block_inv,
    flux_jac,
    face_src,
    send_face,
    elem_route,
    agg_local,
    coarse_block,
    coarse_inv,
):
    elements = rhs.shape[0]
    count = lax.axis_size(("dom", "sub"))
    subs = lax.axis_size("sub")
    owned = coarse_block.shape[0]
    tiles = elements // 128
    pairs = elements // 8
    own = FACES * elements
    far = ROUNDS * 128
    f32, half = jnp.float32, jnp.bfloat16
    dma = pltpu.SemaphoreType.DMA
    result = pl.pallas_call(
        functools.partial(kernel, count, subs),
        out_shape=jax.ShapeDtypeStruct((FLAT, elements), f32),
        in_specs=[pl.BlockSpec(memory_space=pltpu.VMEM)] * 21,
        out_specs=pl.BlockSpec(memory_space=pltpu.VMEM),
        scratch_shapes=[
            pltpu.VMEM((tiles, pairs * PACK_PITCH, 128), f32),
            pltpu.VMEM((tiles, pairs, 128, 128), half),
            pltpu.VMEM((tiles, pairs, 128, 128), half),
            pltpu.VMEM((tiles, pairs * ROW_PITCH, 128), f32),
            pltpu.VMEM((tiles, pairs * ROW_PITCH, 128), f32),
            pltpu.VMEM((tiles, pairs * ROW_PITCH, 128), f32),
            pltpu.VMEM((tiles, pairs * ROW_PITCH, 128), f32),
            pltpu.VMEM((tiles, pairs * ROW_PITCH, 128), f32),
            pltpu.VMEM((FLAT, TRACE), half),
            pltpu.VMEM((own, own), half),
            pltpu.VMEM((far, own), half),
            pltpu.VMEM((own, far), half),
            pltpu.VMEM((FLAT, elements), f32),
            pltpu.VMEM((SIDE, own), f32),
            pltpu.VMEM((SIDE, own), half),
            pltpu.VMEM((SIDE, far), half),
            pltpu.VMEM((TRACE, elements), half),
            pltpu.VMEM((ROUNDS, SIDE, 128), f32),
            pltpu.VMEM((4, ROUNDS, SIDE, 128), f32),
            pltpu.VMEM((count, 8, 128), f32),
            pltpu.VMEM((count, 8, 128), f32),
            pltpu.VMEM((count, 8, 128), f32),
            pltpu.VMEM((count, 8, 128), f32),
            pltpu.VMEM((16, 128), f32),
            pltpu.VMEM((MODES * MODES, owned), f32),
            pltpu.VMEM((MODES * MODES, owned), f32),
            dma((4, ROUNDS)),
            dma((4, ROUNDS)),
            dma((count,)),
            dma((count,)),
            dma((count,)),
            dma((count,)),
        ],
        compiler_params=pltpu.CompilerParams(
            collective_id=0, has_side_effects=True, vmem_limit_bytes=58 * 2**20
        ),
    )(
        rhs.T,
        elem_block.transpose(1, 2, 0),
        block_inv.transpose(1, 2, 0),
        flux_jac,
        face_src.T,
        send_face,
        elem_route.reshape(1, elements),
        agg_local.T,
        coarse_block.transpose(1, 2, 0),
        coarse_inv.transpose(1, 2, 0),
        *const_tables(),
    )
    return result.T


def solution(mesh):
    return jax.shard_map(
        local,
        mesh=mesh,
        in_specs=(
            P(("dom", "sub"), None),
            P(("dom", "sub"), None, None),
            P(("dom", "sub"), None, None),
            P(),
            P(("dom", "sub"), None),
            P(("dom", "sub"), None),
            P(("dom", "sub")),
            P(("dom", "sub"), None),
            P(("dom", "sub"), None, None),
            P(("dom", "sub"), None, None),
        ),
        out_specs=P(("dom", "sub"), None),
        check_vma=False,
    )
```

```python
import functools
import math

import jax
import jax.numpy as jnp
import numpy as np
from jax import lax
from jax.experimental import pallas as pl
from jax.experimental.pallas import tpu as pltpu
from jax.sharding import PartitionSpec as P

COMPS = 13
NODES = 64
FACES = 6
FACE_NODES = 16
MODES = 4
ROUNDS = 5
MOST = 2
FLAT = COMPS * NODES
ROW_PITCH = 40
PACK_PITCH = 136
SIDE = COMPS * FACE_NODES
TRACE = FACES * SIDE

SHORT = 48
PENALTY = 0.5
MESH = pl.DeviceIdType.MESH


def node_tables():
    points = np.array([-1.0, -1.0 / math.sqrt(5.0), 1.0 / math.sqrt(5.0), 1.0])
    weights = np.array([1.0, 5.0, 5.0, 1.0]) / 6.0
    grid_i, grid_j, grid_k = np.meshgrid(points, points, points, indexing="ij")
    weight_grid = weights[:, None, None] * weights[None, :, None] * weights[None, None, :] / 8.0
    basis = np.stack([np.ones(64), grid_i.reshape(-1), grid_j.reshape(-1), grid_k.reshape(-1)])
    restrict = basis * weight_grid.reshape(-1)[None, :]
    number = np.arange(64).reshape(4, 4, 4)
    sides = [number[0], number[3], number[:, 0], number[:, 3], number[:, :, 0], number[:, :, 3]]
    face_index = np.stack([side.reshape(-1) for side in sides])
    return basis, restrict, face_index


def const_tables():
    basis, restrict, face_index = node_tables()
    eye = np.eye(COMPS)
    comp_row = np.pad(np.tile(np.repeat(eye, FACE_NODES, axis=0), (FACES, 1)), ((0, 0), (0, 3))).T
    col_comp = np.pad(np.repeat(eye, NODES, axis=0), ((0, 0), (0, 3)))
    node = np.eye(NODES)[face_index]
    row_node = np.broadcast_to(node[:, None], (FACES, COMPS, FACE_NODES, NODES)).reshape(TRACE, NODES)
    col_node = np.tile(np.eye(NODES), (COMPS, 1))
    select = np.kron(np.eye(2), node.reshape(FACES * FACE_NODES, NODES))
    restrict_t = np.zeros((128, FLAT))
    restrict_t[: COMPS * MODES] = np.kron(eye, restrict)
    basis_t = np.zeros((FLAT, 128))
    basis_t[:, : COMPS * MODES] = np.kron(eye, basis.T)
    to_short = np.zeros((FACES * SHORT, 128))
    from_short = np.zeros((TRACE, SHORT))
    normal = (1, 1, 2, 2, 3, 3)
    tangent = ((2, 3), (2, 3), (1, 3), (1, 3), (1, 2), (1, 2))
    for f in range(FACES):
        for c in range(COMPS):
            row = f * SHORT + 3 * c
            to_short[row, c * MODES] = 1.0
            to_short[row, c * MODES + normal[f]] = -1.0 if f % 2 == 0 else 1.0
            to_short[row + 1, c * MODES + tangent[f][0]] = 1.0
            to_short[row + 2, c * MODES + tangent[f][1]] = 1.0
            rows = slice(f * SIDE + c * FACE_NODES, f * SIDE + (c + 1) * FACE_NODES)
            from_short[rows, 3 * c] = 1.0
            from_short[rows, 3 * c + 1] = basis[tangent[f][0], face_index[f]]
            from_short[rows, 3 * c + 2] = basis[tangent[f][1], face_index[f]]
    pick = np.zeros((128, MODES * 128))
    coef = np.zeros((16, MODES * 128))
    for k in range(MODES):
        for c in range(COMPS):
            for m in range(MODES):
                pick[c * MODES + k, k * 128 + c * MODES + m] = 1.0
                coef[m * MODES + k, k * 128 + c * MODES + m] = 1.0
    half = jnp.bfloat16
    return (
        jnp.asarray(comp_row, half),
        jnp.asarray(row_node.T, half),
        jnp.asarray(col_comp, half),
        jnp.asarray(col_node, half),
        jnp.asarray(select, half),
        jnp.asarray(to_short, half),
        jnp.asarray(from_short, half),
        *parts_of(restrict_t),
        *parts_of(basis_t),
        jnp.asarray(pick, half),
        jnp.asarray(coef, half),
    )


def parts_of(table):
    table = np.asarray(table, np.float32)
    high = table.astype(jnp.bfloat16)
    return jnp.asarray(high), jnp.asarray((table - high.astype(np.float32)).astype(jnp.bfloat16))


def dot(a, b):
    return jnp.dot(a, b, preferred_element_type=jnp.float32)


def general(a, b, dims):
    return lax.dot_general(a, b, (dims, ((), ())), preferred_element_type=jnp.float32)


def split(value):
    high = value.astype(jnp.bfloat16)
    return high, (value - high.astype(jnp.float32)).astype(jnp.bfloat16)


def dot_ones(ones, value, dims=((1,), (0,))):
    high, low = split(value)
    return general(ones, high, dims) + general(ones, low, dims)


def dot_split(value, ones, dims):
    high, low = split(value)
    return general(high, ones, dims) + general(low, ones, dims)


def dot_parts(table, value):
    high, low = split(value)
    return dot(table[0], high) + (dot(table[0], low) + dot(table[1], high))


def kernel(
    count, subs,
    rhs, blocks, inverse, jac, face_src, send_face, route, agg_local, cblock, cinv,
    comp_row, node_row, col_comp, col_node, select, to_short, from_short,
    restrict_high, restrict_low, basis_high, basis_low, pick, coef,
    out,
    stage, block_w, inverse_w, rhs_lam, state, work, resid_lam, delta,
    lift_t, lift_short, restrict_flux_high, restrict_flux_low, pick_local, pick_remote, pick_send,
    lifted, around, near, table, landed, jump, jump_short, sending, arriving,
    bucket, incoming, reply, answer, jac_pad, flat_solve, solve_wide, around_modes,
    send_sem, recv_sem, give_sem, take_sem, back_sem, home_sem,
):
    elements = rhs.shape[1]
    tiles = elements // 128
    own = FACES * elements
    far = ROUNDS * 128
    me = lax.axis_index("dom") * subs + lax.axis_index("sub")

    def place(flat):
        return (flat // subs, flat % subs)

    def partner(k):
        bit = 1 << k
        return me + bit * (1 - 2 * ((me // bit) % 2))

    barrier = pltpu.get_barrier_semaphore()

    def greet(step, carry):
        pl.semaphore_signal(
            barrier, inc=1, device_id=place((me + step) % count), device_id_type=MESH
        )
        return carry

    lax.fori_loop(1, count, greet, 0)

    half_lanes = lax.broadcasted_iota(jnp.int32, (32, 128), 1) < NODES
    pairs = elements // 8

    def pack(source, target):
        def transpose(n, carry):
            rows = source[n].astype(jnp.float32)
            flat = jnp.concatenate([rows[:, :128], rows[:, 128:]], axis=0).T
            for y in range(2):
                even, odd = flat[y * 64 : y * 64 + 32], flat[y * 64 + 32 : y * 64 + 64]
                stage[y, pl.ds(n, pairs, stride=PACK_PITCH), :] = jnp.where(half_lanes, even, odd)
                stage[y, pl.ds(NODES + n, pairs, stride=PACK_PITCH), :] = jnp.where(half_lanes, odd, even)
            return carry

        lax.fori_loop(0, NODES, transpose, 0, unroll=8)

        def cast(j, carry):
            rows = pl.ds(pl.multiple_of(j * PACK_PITCH, 8), 128)
            for y in range(2):
                target[y, j] = stage[y, rows, :].astype(jnp.bfloat16)
            return carry

        lax.fori_loop(0, pairs, cast, 0, unroll=4)

    lane = lax.broadcasted_iota(jnp.int32, (NODES, 128), 1)
    odd_lane = (lane // 32) % 2 == 1

    def to_lam(source, target):
        for c in range(COMPS):
            rows = slice(c * NODES, (c + 1) * NODES)
            low, high = source[rows, :128], source[rows, 128:]
            flat = jnp.concatenate(
                [jnp.where(odd_lane, high, low), jnp.where(odd_lane, low, high)], axis=0
            ).T
            for y in range(2):
                for x in range(2):
                    start = y * 64 + x * 32
                    target[y, pl.ds(16 * x + c, pairs, stride=ROW_PITCH), :] = flat[start : start + 32]

    def from_lam(source, emit):
        for c in range(COMPS):
            flat = jnp.concatenate(
                [
                    source[y, pl.ds(16 * x + c, pairs, stride=ROW_PITCH), :]
                    for y in range(2)
                    for x in range(2)
                ],
                axis=0,
            ).T
            even, odd = flat[:NODES], flat[NODES:]
            rows = slice(c * NODES, (c + 1) * NODES)
            emit(rows, slice(0, 128), jnp.where(odd_lane, odd, even))
            emit(rows, slice(128, 256), jnp.where(odd_lane, even, odd))

    low_half = half_lanes[:16]
    blank = jnp.zeros((16, 128), jnp.float32)

    def apply_blocks(load, weights, emit):
        def body(g, carry):
            for y in range(2):
                parts = []
                for i in range(2):
                    row = pl.multiple_of((2 * g + i) * ROW_PITCH, 8)
                    even = load(y, pl.ds(row, 16))
                    odd = pltpu.roll(load(y, pl.ds(row + 16, 16)), NODES, 1)
                    parts += [
                        jnp.where(low_half, even, blank),
                        jnp.where(low_half, odd, blank),
                        jnp.where(low_half, blank, even),
                        jnp.where(low_half, blank, odd),
                    ]
                left = jnp.concatenate(parts, axis=0).astype(jnp.bfloat16)
                right = weights[y, pl.ds(2 * g, 2)].reshape(256, 128)
                both = lax.dot_general(
                    left, right, (((1,), (1,)), ((), ())), preferred_element_type=jnp.float32
                )
                for i in range(2):
                    row = pl.multiple_of((2 * g + i) * ROW_PITCH, 8)
                    value = both[64 * i : 64 * i + 64, 128 * i : 128 * i + 128]
                    emit(y, pl.ds(row, 16), jnp.where(low_half, value[:16], value[32:48]))
                    emit(y, pl.ds(row + 16, 16), jnp.where(low_half, value[48:], value[16:32]))
            return carry

        lax.fori_loop(0, pairs // 2, body, 0, unroll=8)

    def load_from(source):
        return lambda y, rows: source[y, rows, :]

    def store(target):
        def emit(y, rows, value):
            target[y, rows, :] = value
        return emit

    def add_to(target):
        def emit(y, rows, value):
            target[y, rows, :] = target[y, rows, :] + value
        return emit

    pack(inverse, inverse_w)
    to_lam(rhs, rhs_lam)
    apply_blocks(load_from(rhs_lam), inverse_w, store(state))

    def column(row):
        element = (row * 43691) >> 18
        return jnp.where(row < own, (row - element * FACES) * elements + element, row)

    def one_hot(rows, wanted, value=1.0):
        index = lax.broadcasted_iota(jnp.int32, (rows, wanted.shape[1]), 0)
        return jnp.where(index == wanted, value, 0.0).astype(jnp.bfloat16)

    for k in range(ROUNDS):
        wanted = column(send_face[k : k + 1, :])

        def send_rows(f, carry):
            rows = pl.ds(pl.multiple_of(f * elements, elements), elements)
            pick_send[rows, k * 128 : (k + 1) * 128] = one_hot(elements, wanted - f * elements)
            return carry

        lax.fori_loop(0, FACES, send_rows, 0)

    def local_tables():
        jac_pad[...] = jnp.zeros_like(jac_pad)
        jac_pad[:COMPS, :COMPS] = PENALTY * jac[...]
        spread_jac = general(jac_pad[...].astype(jnp.bfloat16), comp_row[...], ((0,), (0,)))[
            :16
        ].astype(jnp.bfloat16)

        def lifts(i, carry):
            rows = pl.ds(pl.multiple_of(i * 208, 208), 208)
            value = dot(col_comp[rows, :], spread_jac) * dot(col_node[rows, :], node_row[...])
            lift_t[rows, :] = value.astype(jnp.bfloat16)
            return carry

        lax.fori_loop(0, FLAT // 208, lifts, 0)
        row = lax.broadcasted_iota(jnp.int32, (elements, elements), 0)
        mine = jnp.where(row == lax.broadcasted_iota(jnp.int32, (elements, elements), 1), 1.0, 0.0)
        for f in range(FACES):
            lanes = slice(f * elements, (f + 1) * elements)
            wanted = column(face_src[f : f + 1, :])

            def local_rows(g, carry):
                rows = pl.ds(pl.multiple_of(g * elements, elements), elements)
                pick_local[rows, lanes] = one_hot(elements, wanted - g * elements, -1.0)
                return carry

            lax.fori_loop(0, FACES, local_rows, 0)
            pick_local[lanes, lanes] = pick_local[lanes, lanes] + mine.astype(jnp.bfloat16)

            def remote_rows(k, carry):
                rows = pl.ds(pl.multiple_of(k * 128, 128), 128)
                pick_remote[rows, lanes] = one_hot(128, wanted - own - k * 128, -1.0)
                return carry

            lax.fori_loop(0, ROUNDS, remote_rows, 0)

    odd_face = (lax.broadcasted_iota(jnp.int32, (FACES * FACE_NODES, 128), 1) // 32) % 2 == 1

    def traces():
        for c in range(COMPS):
            flat = jnp.concatenate(
                [
                    state[y, pl.ds(16 * x + c, pairs, stride=ROW_PITCH), :]
                    for y in range(2)
                    for x in range(2)
                ],
                axis=0,
            ).astype(jnp.bfloat16)
            value = general(select[...], flat, ((1,), (1,)))
            even, odd = value[: FACES * FACE_NODES], value[FACES * FACE_NODES :]
            low = jnp.where(odd_face, odd, even).astype(jnp.bfloat16)
            high = jnp.where(odd_face, even, odd).astype(jnp.bfloat16)
            rows = slice(c * FACE_NODES, (c + 1) * FACE_NODES)
            for f in range(FACES):
                part = slice(f * FACE_NODES, (f + 1) * FACE_NODES)
                table[rows, f * elements : f * elements + 128] = low[part]
                table[rows, f * elements + 128 : (f + 1) * elements] = high[part]

    def begin(number, rows):
        copies = {}
        for group in ((4, 3), (2, 1, 0)):
            lanes = slice(min(group) * 128, (max(group) + 1) * 128)
            outgoing = dot(table[:rows, :], pick_send[:, lanes])
            for k in group:
                start = (k - min(group)) * 128
                sending[k, :rows, :] = outgoing[:, start : start + 128]
                copies[k] = pltpu.make_async_remote_copy(
                    src_ref=sending.at[k, pl.ds(0, rows)],
                    dst_ref=arriving.at[number, k, pl.ds(0, rows)],
                    send_sem=send_sem.at[number, k],
                    recv_sem=recv_sem.at[number, k],
                    device_id=place(partner(k)),
                    device_id_type=MESH,
                )
                copies[k].start()
        return copies

    def end(number, rows, copies, target):
        def land(k):
            copies[k].wait_recv()
            landed[:rows, k * 128 : (k + 1) * 128] = arriving[number, k, :rows, :].astype(
                jnp.bfloat16
            )

        for k in (0, 1, 2):
            land(k)
        near[:rows, :] = near[:rows, :] + dot(landed[:rows, : 3 * 128], pick_remote[: 3 * 128, :])
        for k in (3, 4):
            land(k)
        value = near[:rows, :] + dot(landed[:rows, 3 * 128 :], pick_remote[3 * 128 :, :])
        for f in range(FACES):
            target[f * rows : (f + 1) * rows, :] = value[:, f * elements : (f + 1) * elements].astype(
                jnp.bfloat16
            )
        for k in range(ROUNDS):
            copies[k].wait_send()

    def operate(number, between=None, beside=None):
        traces()
        copies = begin(number, SIDE)
        if between is not None:
            between()
        near[...] = dot(table[...], pick_local[...])
        apply_blocks(load_from(state), block_w, store(work))
        if beside is not None:
            beside()
        end(number, SIDE, copies, jump)

    def residual(y, rows):
        return rhs_lam[y, rows, :] - work[y, rows, :] - delta[y, rows, :]

    def sweep(number, between=None):
        operate(number, between)
        lifted[...] = dot(lift_t[...], jump[...])
        to_lam(lifted, delta)
        apply_blocks(residual, inverse_w, add_to(state))

    def exchange(source, target, sent, got, between=None):
        def copy_of(step):
            other = (me + step) % count
            return pltpu.make_async_remote_copy(
                src_ref=source.at[other, pl.ds(0, MOST)],
                dst_ref=target.at[me, pl.ds(0, MOST)],
                send_sem=sent,
                recv_sem=got,
                device_id=place(other),
                device_id_type=MESH,
            )

        def start(step, carry):
            copy_of(step).start()
            return carry

        lax.fori_loop(1, count, start, 0, unroll=4)
        target[me] = source[me]
        if between is not None:
            between()
        everything = pl.ds(0, count - 1), pl.ds(0, MOST)
        for semaphore in (got, sent):
            pltpu.make_async_copy(source.at[everything], target.at[everything], semaphore).wait()

    def behind_first():
        local_tables()
        pack(blocks, block_w)

    owned = cblock.shape[2]
    inverse_rows = [cinv[m] for m in range(MODES)]
    block_rows = [cblock[m] for m in range(MODES)]

    def times(rows, k, other):
        return rows[k : k + 1, :] * other

    def solve_rows():
        inner = [
            sum(times(block_rows[p], q, inverse_rows[q]) for q in range(MODES)) for p in range(MODES)
        ]
        for m in range(MODES):
            flat_solve[m * MODES : (m + 1) * MODES, :] = 2.0 * inverse_rows[m] - sum(
                times(inverse_rows[m], p, inner[p]) for p in range(MODES)
            )

    solve_rows()
    pl.semaphore_wait(barrier, count - 1)
    sweep(0, behind_first)

    def behind_second():
        def emit_around(rows, lanes, value):
            around[rows, lanes] = rhs[rows, lanes] - value

        from_lam(work, emit_around)
        around_modes[...] = dot_parts((restrict_high[...], restrict_low[...]), around[...])
        for f in range(FACES):
            rows = slice(f * SIDE, (f + 1) * SIDE)
            lift_short[:, f * SHORT : (f + 1) * SHORT] = dot(
                lift_t[:, rows], from_short[rows, :]
            ).astype(jnp.bfloat16)
        high, low = split(
            dot(restrict_high[...], lift_t[...]) + dot(restrict_low[...], lift_t[...])
        )
        restrict_flux_high[...] = high
        restrict_flux_low[...] = low
        solve_wide[...] = dot_split(flat_solve[...], coef[...], ((0,), (0,)))

    operate(1, beside=behind_second)
    partial = around_modes[...] - (
        dot(restrict_flux_high[...], jump[...]) + dot(restrict_flux_low[...], jump[...])
    )
    route_row = (route[...] // MOST) * 8 + route[...] % MOST
    to_bucket = one_hot(count * 8, route_row)
    bucket[...] = dot_ones(to_bucket, partial, ((1,), (1,))).reshape(count, 8, 128)

    def behind_bucket():
        lifted[...] = dot(lift_t[...], jump[...])
        to_lam(lifted, delta)
        resid_lam[...] = rhs_lam[...] - work[...] - delta[...]

    exchange(bucket, incoming, give_sem, take_sem, behind_bucket)
    members = [one_hot(owned, agg_local[s : s + 1, :]) for s in range(MOST)]
    coarse_rhs = sum(dot_ones(members[s], incoming[:, s, :]) for s in range(MOST))
    product = solve_wide[...] * dot_split(coarse_rhs, pick[...], ((1,), (0,)))
    solved = product[:, :128] + product[:, 128:256] + product[:, 256:384] + product[:, 384:]
    reply[...] = jnp.zeros_like(reply)
    for s in range(MOST):
        reply[:, s, :] = dot_ones(members[s], solved, ((0,), (0,)))
    exchange(reply, answer, back_sem, home_sem)
    slot = lax.broadcasted_iota(jnp.int32, (count * 8, 128), 0) % 8
    returned = jnp.where(slot < MOST, answer[...].reshape(count * 8, 128), 0.0)
    correction = dot_split(returned, to_bucket, ((0,), (0,)))

    short = dot_ones(to_short[...], correction).astype(jnp.bfloat16)
    for f in range(FACES):
        table[:SHORT, f * elements : (f + 1) * elements] = short[f * SHORT : (f + 1) * SHORT]
    copies = begin(2, SHORT)
    lifted[...] = dot_parts((basis_high[...], basis_low[...]), correction)
    to_lam(lifted, delta)
    state[...] = state[...] + delta[...]
    apply_blocks(load_from(delta), block_w, store(work))
    resid_lam[...] = resid_lam[...] - work[...]
    near[:SHORT, :] = dot(table[:SHORT, :], pick_local[...])
    end(2, SHORT, copies, jump_short)
    lifted[...] = dot(lift_short[...], jump_short[...])
    to_lam(lifted, delta)

    def coarse_residual(y, rows):
        return resid_lam[y, rows, :] - delta[y, rows, :]

    apply_blocks(coarse_residual, inverse_w, add_to(state))
    sweep(3)

    def emit_out(rows, lanes, value):
        out[rows, lanes] = value

    from_lam(state, emit_out)


def local(
    rhs,
    elem_block,
    block_inv,
    flux_jac,
    face_src,
    send_face,
    elem_route,
    agg_local,
    coarse_block,
    coarse_inv,
):
    elements = rhs.shape[0]
    count = lax.axis_size(("dom", "sub"))
    subs = lax.axis_size("sub")
    owned = coarse_block.shape[0]
    tiles = elements // 128
    pairs = elements // 8
    own = FACES * elements
    far = ROUNDS * 128
    f32, half = jnp.float32, jnp.bfloat16
    dma = pltpu.SemaphoreType.DMA
    result = pl.pallas_call(
        functools.partial(kernel, count, subs),
        out_shape=jax.ShapeDtypeStruct((FLAT, elements), f32),
        in_specs=[pl.BlockSpec(memory_space=pltpu.VMEM)] * 23,
        out_specs=pl.BlockSpec(memory_space=pltpu.VMEM),
        scratch_shapes=[
            pltpu.VMEM((tiles, pairs * PACK_PITCH, 128), f32),
            pltpu.VMEM((tiles, pairs, 128, 128), half),
            pltpu.VMEM((tiles, pairs, 128, 128), half),
            pltpu.VMEM((tiles, pairs * ROW_PITCH, 128), f32),
            pltpu.VMEM((tiles, pairs * ROW_PITCH, 128), f32),
            pltpu.VMEM((tiles, pairs * ROW_PITCH, 128), f32),
            pltpu.VMEM((tiles, pairs * ROW_PITCH, 128), f32),
            pltpu.VMEM((tiles, pairs * ROW_PITCH, 128), f32),
            pltpu.VMEM((FLAT, TRACE), half),
            pltpu.VMEM((FLAT, FACES * SHORT), half),
            pltpu.VMEM((128, TRACE), half),
            pltpu.VMEM((128, TRACE), half),
            pltpu.VMEM((own, own), half),
            pltpu.VMEM((far, own), half),
            pltpu.VMEM((own, far), half),
            pltpu.VMEM((FLAT, elements), f32),
            pltpu.VMEM((FLAT, elements), f32),
            pltpu.VMEM((SIDE, own), f32),
            pltpu.VMEM((SIDE, own), half),
            pltpu.VMEM((SIDE, far), half),
            pltpu.VMEM((TRACE, elements), half),
            pltpu.VMEM((FACES * SHORT, elements), half),
            pltpu.VMEM((ROUNDS, SIDE, 128), f32),
            pltpu.VMEM((4, ROUNDS, SIDE, 128), f32),
            pltpu.VMEM((count, 8, 128), f32),
            pltpu.VMEM((count, 8, 128), f32),
            pltpu.VMEM((count, 8, 128), f32),
            pltpu.VMEM((count, 8, 128), f32),
            pltpu.VMEM((16, 128), f32),
            pltpu.VMEM((MODES * MODES, owned), f32),
            pltpu.VMEM((owned, MODES * 128), f32),
            pltpu.VMEM((128, elements), f32),
            dma((4, ROUNDS)),
            dma((4, ROUNDS)),
            dma,
            dma,
            dma,
            dma,
        ],
        compiler_params=pltpu.CompilerParams(
            collective_id=0, has_side_effects=True, vmem_limit_bytes=58 * 2**20
        ),
    )(
        rhs.T,
        elem_block.transpose(1, 2, 0),
        block_inv.transpose(1, 2, 0),
        flux_jac,
        face_src.T,
        send_face,
        elem_route.reshape(1, elements),
        agg_local.T,
        coarse_block.transpose(1, 2, 0),
        coarse_inv.transpose(1, 2, 0),
        *const_tables(),
    )
    return result.T


def solution(mesh):
    return jax.shard_map(
        local,
        mesh=mesh,
        in_specs=(
            P(("dom", "sub"), None),
            P(("dom", "sub"), None, None),
            P(("dom", "sub"), None, None),
            P(),
            P(("dom", "sub"), None),
            P(("dom", "sub"), None),
            P(("dom", "sub")),
            P(("dom", "sub"), None),
            P(("dom", "sub"), None, None),
            P(("dom", "sub"), None, None),
        ),
        out_specs=P(("dom", "sub"), None),
        check_vma=False,
    )
```

```python
import functools
import math

import jax
import jax.numpy as jnp
import numpy as np
from jax import lax
from jax.experimental import pallas as pl
from jax.experimental.pallas import tpu as pltpu
from jax.sharding import PartitionSpec as P

COMPS = 13
NODES = 64
FACES = 6
FACE_NODES = 16
MODES = 4
ROUNDS = 5
MOST = 2
FLAT = COMPS * NODES
ROW_PITCH = 40
PACK_PITCH = 136
SIDE = COMPS * FACE_NODES
TRACE = FACES * SIDE

SHORT = 48
WHOLE = (0, COMPS)
PIECES = ((0, 8), (8, COMPS))
PENALTY = 0.5
MESH = pl.DeviceIdType.MESH


def node_tables():
    points = np.array([-1.0, -1.0 / math.sqrt(5.0), 1.0 / math.sqrt(5.0), 1.0])
    weights = np.array([1.0, 5.0, 5.0, 1.0]) / 6.0
    grid_i, grid_j, grid_k = np.meshgrid(points, points, points, indexing="ij")
    weight_grid = weights[:, None, None] * weights[None, :, None] * weights[None, None, :] / 8.0
    basis = np.stack([np.ones(64), grid_i.reshape(-1), grid_j.reshape(-1), grid_k.reshape(-1)])
    restrict = basis * weight_grid.reshape(-1)[None, :]
    number = np.arange(64).reshape(4, 4, 4)
    sides = [number[0], number[3], number[:, 0], number[:, 3], number[:, :, 0], number[:, :, 3]]
    face_index = np.stack([side.reshape(-1) for side in sides])
    return basis, restrict, face_index


def const_tables():
    basis, restrict, face_index = node_tables()
    eye = np.eye(COMPS)
    spread = np.pad(np.repeat(eye, FACE_NODES, axis=0), ((0, 0), (0, 3)))
    spread_short = np.pad(np.repeat(eye, 3, axis=0), ((0, SHORT - 3 * COMPS), (0, 3)))
    same = np.kron(np.ones((COMPS, COMPS)), np.eye(FACE_NODES))
    same_short = np.kron(np.ones((SHORT // 3, SHORT // 3)), np.eye(3))
    node = np.eye(NODES)[face_index]
    select = np.kron(np.eye(2), node.reshape(FACES * FACE_NODES, NODES))
    restrict_t = np.zeros((128, FLAT))
    restrict_t[: COMPS * MODES] = np.kron(eye, restrict)
    flux_modes = np.zeros((128, TRACE))
    for f in range(FACES):
        columns = slice(f * SIDE, (f + 1) * SIDE)
        flux_modes[: COMPS * MODES, columns] = np.kron(eye, restrict[:, face_index[f]])
    basis_t = np.zeros((FLAT, 128))
    basis_t[:, : COMPS * MODES] = np.kron(eye, basis.T)
    to_short = np.zeros((FACES * SHORT, 128))
    from_short = np.zeros((SIDE, SHORT))
    normal = (1, 1, 2, 2, 3, 3)
    tangent = ((2, 3), (2, 3), (1, 3), (1, 3), (1, 2), (1, 2))
    for f in range(FACES):
        for c in range(COMPS):
            row = f * SHORT + 3 * c
            to_short[row, c * MODES] = 1.0
            to_short[row, c * MODES + normal[f]] = -1.0 if f % 2 == 0 else 1.0
            to_short[row + 1, c * MODES + tangent[f][0]] = 1.0
            to_short[row + 2, c * MODES + tangent[f][1]] = 1.0
    for c in range(COMPS):
        rows = slice(c * FACE_NODES, (c + 1) * FACE_NODES)
        from_short[rows, 3 * c] = 1.0
        from_short[rows, 3 * c + 1] = basis[2, face_index[0]]
        from_short[rows, 3 * c + 2] = basis[3, face_index[0]]
    pick = np.zeros((128, MODES * 128))
    coef = np.zeros((16, MODES * 128))
    for k in range(MODES):
        for c in range(COMPS):
            for m in range(MODES):
                pick[c * MODES + k, k * 128 + c * MODES + m] = 1.0
                coef[m * MODES + k, k * 128 + c * MODES + m] = 1.0
    half = jnp.bfloat16
    return (
        jnp.asarray(spread, half),
        jnp.asarray(spread_short, half),
        jnp.asarray(same, half),
        jnp.asarray(same_short, half),
        jnp.asarray(select, half),
        jnp.asarray(to_short, half),
        jnp.asarray(from_short, half),
        *parts_of(restrict_t),
        *parts_of(flux_modes),
        *parts_of(basis_t),
        jnp.asarray(pick, half),
        jnp.asarray(coef, half),
    )


def parts_of(table):
    table = np.asarray(table, np.float32)
    high = table.astype(jnp.bfloat16)
    return jnp.asarray(high), jnp.asarray((table - high.astype(np.float32)).astype(jnp.bfloat16))


def dot(a, b):
    return jnp.dot(a, b, preferred_element_type=jnp.float32)


def general(a, b, dims):
    return lax.dot_general(a, b, (dims, ((), ())), preferred_element_type=jnp.float32)


def split(value):
    high = value.astype(jnp.bfloat16)
    return high, (value - high.astype(jnp.float32)).astype(jnp.bfloat16)


def dot_ones(ones, value, dims=((1,), (0,))):
    high, low = split(value)
    return general(ones, high, dims) + general(ones, low, dims)


def dot_split(value, ones, dims):
    high, low = split(value)
    return general(high, ones, dims) + general(low, ones, dims)


def dot_parts(table, value):
    high, low = split(value)
    return dot(table[0], high) + (dot(table[0], low) + dot(table[1], high))


def kernel(
    count, subs,
    rhs, blocks, inverse, jac, face_src, send_face, route, agg_local, cblock, cinv,
    spread, spread_short, same, same_short, select, to_short, from_short,
    restrict_high, restrict_low, flux_high, flux_low, basis_high, basis_low, pick, coef,
    out,
    stage, block_w, inverse_w, rhs_lam, state, work, resid_lam, delta,
    mixer, mixer_short, pick_local, pick_remote, pick_send,
    lifted, around, near, table, landed, jump, sending, arriving,
    bucket, incoming, reply, answer, jac_pad, flat_solve, solve_wide, around_modes,
    send_sem, recv_sem, give_sem, take_sem, back_sem, home_sem,
):
    elements = rhs.shape[1]
    tiles = elements // 128
    own = FACES * elements
    far = ROUNDS * 128
    me = lax.axis_index("dom") * subs + lax.axis_index("sub")

    def place(flat):
        return (flat // subs, flat % subs)

    def partner(k):
        bit = 1 << k
        return me + bit * (1 - 2 * ((me // bit) % 2))

    barrier = pltpu.get_barrier_semaphore()

    def greet(step, carry):
        pl.semaphore_signal(
            barrier, inc=1, device_id=place((me + step) % count), device_id_type=MESH
        )
        return carry

    lax.fori_loop(1, count, greet, 0)

    half_lanes = lax.broadcasted_iota(jnp.int32, (32, 128), 1) < NODES
    pairs = elements // 8

    def pack(source, target):
        def transpose(n, carry):
            rows = source[n].astype(jnp.float32)
            flat = jnp.concatenate([rows[:, :128], rows[:, 128:]], axis=0).T
            for y in range(2):
                even, odd = flat[y * 64 : y * 64 + 32], flat[y * 64 + 32 : y * 64 + 64]
                stage[y, pl.ds(n, pairs, stride=PACK_PITCH), :] = jnp.where(half_lanes, even, odd)
                stage[y, pl.ds(NODES + n, pairs, stride=PACK_PITCH), :] = jnp.where(half_lanes, odd, even)
            return carry

        lax.fori_loop(0, NODES, transpose, 0, unroll=8)

        def cast(j, carry):
            rows = pl.ds(pl.multiple_of(j * PACK_PITCH, 8), 128)
            for y in range(2):
                target[y, j] = stage[y, rows, :].astype(jnp.bfloat16)
            return carry

        lax.fori_loop(0, pairs, cast, 0, unroll=4)

    lane = lax.broadcasted_iota(jnp.int32, (NODES, 128), 1)
    odd_lane = (lane // 32) % 2 == 1

    def to_lam(source, target):
        for c in range(COMPS):
            rows = slice(c * NODES, (c + 1) * NODES)
            low, high = source[rows, :128], source[rows, 128:]
            flat = jnp.concatenate(
                [jnp.where(odd_lane, high, low), jnp.where(odd_lane, low, high)], axis=0
            ).T
            for y in range(2):
                for x in range(2):
                    start = y * 64 + x * 32
                    target[y, pl.ds(16 * x + c, pairs, stride=ROW_PITCH), :] = flat[start : start + 32]

    def from_lam(source, emit, comps=WHOLE):
        for c in range(*comps):
            flat = jnp.concatenate(
                [
                    source[y, pl.ds(16 * x + c, pairs, stride=ROW_PITCH), :]
                    for y in range(2)
                    for x in range(2)
                ],
                axis=0,
            ).T
            even, odd = flat[:NODES], flat[NODES:]
            rows = slice(c * NODES, (c + 1) * NODES)
            emit(rows, slice(0, 128), jnp.where(odd_lane, odd, even))
            emit(rows, slice(128, 256), jnp.where(odd_lane, even, odd))

    low_half = half_lanes[:16]
    blank = jnp.zeros((16, 128), jnp.float32)

    def apply_blocks(load, weights, emit):
        def body(g, carry):
            for y in range(2):
                parts = []
                for i in range(2):
                    row = pl.multiple_of((2 * g + i) * ROW_PITCH, 8)
                    even = load(y, pl.ds(row, 16))
                    odd = pltpu.roll(load(y, pl.ds(row + 16, 16)), NODES, 1)
                    parts += [
                        jnp.where(low_half, even, blank),
                        jnp.where(low_half, odd, blank),
                        jnp.where(low_half, blank, even),
                        jnp.where(low_half, blank, odd),
                    ]
                left = jnp.concatenate(parts, axis=0).astype(jnp.bfloat16)
                right = weights[y, pl.ds(2 * g, 2)].reshape(256, 128)
                both = lax.dot_general(
                    left, right, (((1,), (1,)), ((), ())), preferred_element_type=jnp.float32
                )
                for i in range(2):
                    row = pl.multiple_of((2 * g + i) * ROW_PITCH, 8)
                    value = both[64 * i : 64 * i + 64, 128 * i : 128 * i + 128]
                    emit(y, pl.ds(row, 16), jnp.where(low_half, value[:16], value[32:48]))
                    emit(y, pl.ds(row + 16, 16), jnp.where(low_half, value[48:], value[16:32]))
            return carry

        lax.fori_loop(0, pairs // 2, body, 0, unroll=8)

    low_eight = half_lanes[:8]
    blank_eight = jnp.zeros((8, 128), jnp.float32)

    def apply_part(load, weights, emit, first):
        def body(g, carry):
            for y in range(2):
                parts = []
                for i in range(2):
                    row = pl.multiple_of((2 * g + i) * ROW_PITCH + first, 8)
                    even = load(y, pl.ds(row, 8))
                    odd = pltpu.roll(load(y, pl.ds(row + 16, 8)), NODES, 1)
                    parts += [
                        jnp.where(low_eight, even, blank_eight),
                        jnp.where(low_eight, odd, blank_eight),
                        jnp.where(low_eight, blank_eight, even),
                        jnp.where(low_eight, blank_eight, odd),
                    ]
                left = jnp.concatenate(parts, axis=0).astype(jnp.bfloat16)
                right = weights[y, pl.ds(2 * g, 2)].reshape(256, 128)
                both = general(left, right, ((1,), (1,)))
                for i in range(2):
                    row = pl.multiple_of((2 * g + i) * ROW_PITCH + first, 8)
                    value = both[32 * i : 32 * i + 32, 128 * i : 128 * i + 128]
                    emit(y, pl.ds(row, 8), jnp.where(low_eight, value[:8], value[16:24]))
                    emit(y, pl.ds(row + 16, 8), jnp.where(low_eight, value[24:], value[8:16]))
            return carry

        lax.fori_loop(0, pairs // 2, body, 0, unroll=8)

    def load_from(source):
        return lambda y, rows: source[y, rows, :]

    def store(target):
        def emit(y, rows, value):
            target[y, rows, :] = value
        return emit

    def add_to(target):
        def emit(y, rows, value):
            target[y, rows, :] = target[y, rows, :] + value
        return emit

    pack(inverse, inverse_w)
    to_lam(rhs, rhs_lam)
    apply_blocks(load_from(rhs_lam), inverse_w, store(state))

    def column(row):
        element = (row * 43691) >> 18
        return jnp.where(row < own, (row - element * FACES) * elements + element, row)

    def one_hot(rows, wanted, value=1.0):
        index = lax.broadcasted_iota(jnp.int32, (rows, wanted.shape[1]), 0)
        return jnp.where(index == wanted, value, 0.0).astype(jnp.bfloat16)

    for k in range(ROUNDS):
        wanted = column(send_face[k : k + 1, :])

        def send_rows(f, carry):
            rows = pl.ds(pl.multiple_of(f * elements, elements), elements)
            pick_send[rows, k * 128 : (k + 1) * 128] = one_hot(elements, wanted - f * elements)
            return carry

        lax.fori_loop(0, FACES, send_rows, 0)

    jac_pad[...] = jnp.zeros_like(jac_pad)
    jac_pad[:COMPS, :COMPS] = PENALTY * jac[...]
    jac_half = jac_pad[...].astype(jnp.bfloat16)
    for rows, mask, target in ((spread, same, mixer), (spread_short, same_short, mixer_short)):
        half_way = general(rows[...], jac_half, ((1,), (1,))).astype(jnp.bfloat16)
        value = general(half_way, rows[...], ((1,), (1,))) * mask[...].astype(jnp.float32)
        target[...] = value.astype(jnp.bfloat16)

    def local_tables():
        row = lax.broadcasted_iota(jnp.int32, (elements, elements), 0)
        mine = jnp.where(row == lax.broadcasted_iota(jnp.int32, (elements, elements), 1), 1.0, 0.0)
        for f in range(FACES):
            lanes = slice(f * elements, (f + 1) * elements)
            wanted = column(face_src[f : f + 1, :])

            def local_rows(g, carry):
                rows = pl.ds(pl.multiple_of(g * elements, elements), elements)
                pick_local[rows, lanes] = one_hot(elements, wanted - g * elements, -1.0)
                return carry

            lax.fori_loop(0, FACES, local_rows, 0)
            pick_local[lanes, lanes] = pick_local[lanes, lanes] + mine.astype(jnp.bfloat16)

            def remote_rows(k, carry):
                rows = pl.ds(pl.multiple_of(k * 128, 128), 128)
                pick_remote[rows, lanes] = one_hot(128, wanted - own - k * 128, -1.0)
                return carry

            lax.fori_loop(0, ROUNDS, remote_rows, 0)

    odd_face = (lax.broadcasted_iota(jnp.int32, (FACES * FACE_NODES, 128), 1) // 32) % 2 == 1

    def traces(comps):
        for c in range(*comps):
            flat = jnp.concatenate(
                [
                    state[y, pl.ds(16 * x + c, pairs, stride=ROW_PITCH), :]
                    for y in range(2)
                    for x in range(2)
                ],
                axis=0,
            ).astype(jnp.bfloat16)
            value = general(select[...], flat, ((1,), (1,)))
            even, odd = value[: FACES * FACE_NODES], value[FACES * FACE_NODES :]
            low = jnp.where(odd_face, odd, even).astype(jnp.bfloat16)
            high = jnp.where(odd_face, even, odd).astype(jnp.bfloat16)
            rows = slice(c * FACE_NODES, (c + 1) * FACE_NODES)
            for f in range(FACES):
                part = slice(f * FACE_NODES, (f + 1) * FACE_NODES)
                table[rows, f * elements : f * elements + 128] = low[part]
                table[rows, f * elements + 128 : (f + 1) * elements] = high[part]

    def begin(number, rows, mix, pieces):
        copies = {}
        for group in ((4, 3), (2, 1, 0)):
            lanes = slice(min(group) * 128, (max(group) + 1) * 128)
            outgoing = dot(table[:rows, :], pick_send[:, lanes]).astype(jnp.bfloat16)
            for piece, (low, high) in enumerate(pieces if 4 in group else ((0, rows),)):
                mixed = dot(mix[low:high, :], outgoing)
                for k in group:
                    start = (k - min(group)) * 128
                    sending[k, low:high, :] = mixed[:, start : start + 128]
                    copies[k, piece] = pltpu.make_async_remote_copy(
                        src_ref=sending.at[k, pl.ds(low, high - low)],
                        dst_ref=arriving.at[number, k, pl.ds(low, high - low)],
                        send_sem=send_sem.at[number, k, piece],
                        recv_sem=recv_sem.at[number, k, piece],
                        device_id=place(partner(k)),
                        device_id_type=MESH,
                    )
                    copies[k, piece].start()
        return copies

    def land(number, copies, k, piece, low, high):
        copies[k, piece].wait_recv()
        landed[low:high, k * 128 : (k + 1) * 128] = arriving[number, k, low:high, :].astype(
            jnp.bfloat16
        )

    def surround(number, copies, rows, mix):
        beside = dot(table[:rows, :], pick_local[...]).astype(jnp.bfloat16)
        near[:rows, :] = dot(mix[...], beside)
        return beside

    def first_rounds(number, copies, rows):
        for k in (0, 1, 2):
            land(number, copies, k, 0, 0, rows)
        return near[:rows, :] + dot(landed[:rows, : 3 * 128], pick_remote[: 3 * 128, :])

    def last_rounds(number, copies, piece, low, high):
        for k in (3, 4):
            land(number, copies, k, piece, low, high)
        return dot(landed[low:high, 3 * 128 :], pick_remote[3 * 128 :, :])

    def scatter(comps):
        for c in range(*comps):
            rows = slice(c * FACE_NODES, (c + 1) * FACE_NODES)
            stack = jnp.concatenate(
                [
                    jump[rows, f * elements + 128 * h : f * elements + 128 * (h + 1)]
                    for h in range(2)
                    for f in range(FACES)
                ],
                axis=0,
            )
            flat = general(stack, select[...], ((0,), (0,)))
            for y in range(2):
                even, odd = flat[y * 64 : y * 64 + 32], flat[y * 64 + 32 : y * 64 + 64]
                delta[y, pl.ds(c, pairs, stride=ROW_PITCH), :] = even
                delta[y, pl.ds(16 + c, pairs, stride=ROW_PITCH), :] = pltpu.roll(odd, NODES, 1)

    side_pieces = tuple((low * FACE_NODES, high * FACE_NODES) for low, high in PIECES)

    def operate(number, between=None):
        copies = begin(number, SIDE, mixer, side_pieces)
        if between is not None:
            between()
        surround(number, copies, SIDE, mixer)
        apply_blocks(load_from(state), block_w, store(work))
        jump[...] = first_rounds(number, copies, SIDE).astype(jnp.bfloat16)
        scatter(WHOLE)
        resid_lam[...] = rhs_lam[...] - work[...] - delta[...]
        return copies

    def residual(y, rows):
        return resid_lam[y, rows, :] - delta[y, rows, :]

    def gather_piece(number, copies, piece):
        low, high = side_pieces[piece]
        jump[low:high, :] = last_rounds(number, copies, piece, low, high).astype(jnp.bfloat16)

    def leave(copies):
        for copy in copies.values():
            copy.wait_send()

    def sweep(number, after, between=None):
        copies = operate(number, between)
        for piece, comps in enumerate(PIECES):
            gather_piece(number, copies, piece)
            scatter(comps)
            apply_part(residual, inverse_w, add_to(state), comps[0])
            after(comps)
        leave(copies)

    def exchange(source, target, sent, got, between=None):
        def copy_of(step):
            other = (me + step) % count
            return pltpu.make_async_remote_copy(
                src_ref=source.at[other, pl.ds(0, MOST)],
                dst_ref=target.at[me, pl.ds(0, MOST)],
                send_sem=sent,
                recv_sem=got,
                device_id=place(other),
                device_id_type=MESH,
            )

        def start(step, carry):
            copy_of(step).start()
            return carry

        lax.fori_loop(1, count, start, 0, unroll=4)
        target[me] = source[me]
        if between is not None:
            between()
        everything = pl.ds(0, count - 1), pl.ds(0, MOST)
        for semaphore in (got, sent):
            pltpu.make_async_copy(source.at[everything], target.at[everything], semaphore).wait()

    def behind_first():
        local_tables()
        pack(blocks, block_w)

    owned = cblock.shape[2]
    inverse_rows = [cinv[m] for m in range(MODES)]
    block_rows = [cblock[m] for m in range(MODES)]

    def times(rows, k, other):
        return rows[k : k + 1, :] * other

    def solve_rows():
        inner = [
            sum(times(block_rows[p], q, inverse_rows[q]) for q in range(MODES)) for p in range(MODES)
        ]
        for m in range(MODES):
            flat_solve[m * MODES : (m + 1) * MODES, :] = 2.0 * inverse_rows[m] - sum(
                times(inverse_rows[m], p, inner[p]) for p in range(MODES)
            )

    solve_rows()
    pl.semaphore_wait(barrier, count - 1)
    traces(WHOLE)
    sweep(0, traces, behind_first)
    copies = operate(1)

    def emit_around(rows, lanes, value):
        around[rows, lanes] = value

    from_lam(resid_lam, emit_around)
    around_modes[...] = dot_parts((restrict_high[...], restrict_low[...]), around[...])
    solve_wide[...] = dot_split(flat_solve[...], coef[...], ((0,), (0,)))
    for piece in range(len(PIECES)):
        gather_piece(1, copies, piece)
    leave(copies)
    restricted = jnp.zeros((128, elements), jnp.float32)
    for f in range(FACES):
        columns = slice(f * SIDE, (f + 1) * SIDE)
        side = jump[:, f * elements : (f + 1) * elements]
        restricted += dot(flux_high[:, columns], side) + dot(flux_low[:, columns], side)
    partial = around_modes[...] - restricted
    route_row = (route[...] // MOST) * 8 + route[...] % MOST
    to_bucket = one_hot(count * 8, route_row)
    bucket[...] = dot_ones(to_bucket, partial, ((1,), (1,))).reshape(count, 8, 128)

    def behind_bucket():
        scatter(WHOLE)
        resid_lam[...] = resid_lam[...] - delta[...]

    exchange(bucket, incoming, give_sem, take_sem, behind_bucket)
    members = [one_hot(owned, agg_local[s : s + 1, :]) for s in range(MOST)]
    coarse_rhs = sum(dot_ones(members[s], incoming[:, s, :]) for s in range(MOST))
    product = solve_wide[...] * dot_split(coarse_rhs, pick[...], ((1,), (0,)))
    solved = product[:, :128] + product[:, 128:256] + product[:, 256:384] + product[:, 384:]
    reply[...] = jnp.zeros_like(reply)
    for s in range(MOST):
        reply[:, s, :] = dot_ones(members[s], solved, ((0,), (0,)))
    exchange(reply, answer, back_sem, home_sem)
    slot = lax.broadcasted_iota(jnp.int32, (count * 8, 128), 0) % 8
    returned = jnp.where(slot < MOST, answer[...].reshape(count * 8, 128), 0.0)
    correction = dot_split(returned, to_bucket, ((0,), (0,)))

    short = dot_ones(to_short[...], correction).astype(jnp.bfloat16)
    for f in range(FACES):
        table[:SHORT, f * elements : (f + 1) * elements] = short[f * SHORT : (f + 1) * SHORT]
    copies = begin(2, SHORT, mixer_short, ((0, SHORT),))
    lifted[...] = dot_parts((basis_high[...], basis_low[...]), correction)
    to_lam(lifted, delta)
    state[...] = state[...] + delta[...]
    apply_blocks(load_from(delta), block_w, store(work))
    resid_lam[...] = resid_lam[...] - work[...]
    surround(2, copies, SHORT, mixer_short)
    gathered = first_rounds(2, copies, SHORT) + last_rounds(2, copies, 0, 0, SHORT)
    leave(copies)
    jump[...] = dot(from_short[...], gathered.astype(jnp.bfloat16)).astype(jnp.bfloat16)
    scatter(WHOLE)
    apply_blocks(residual, inverse_w, add_to(state))
    traces(WHOLE)

    def emit_out(rows, lanes, value):
        out[rows, lanes] = value

    def write_out(comps):
        from_lam(state, emit_out, comps)

    sweep(3, write_out)


def local(
    rhs,
    elem_block,
    block_inv,
    flux_jac,
    face_src,
    send_face,
    elem_route,
    agg_local,
    coarse_block,
    coarse_inv,
):
    elements = rhs.shape[0]
    count = lax.axis_size(("dom", "sub"))
    subs = lax.axis_size("sub")
    owned = coarse_block.shape[0]
    tiles = elements // 128
    pairs = elements // 8
    own = FACES * elements
    far = ROUNDS * 128
    f32, half = jnp.float32, jnp.bfloat16
    dma = pltpu.SemaphoreType.DMA
    result = pl.pallas_call(
        functools.partial(kernel, count, subs),
        out_shape=jax.ShapeDtypeStruct((FLAT, elements), f32),
        in_specs=[pl.BlockSpec(memory_space=pltpu.VMEM)] * 25,
        out_specs=pl.BlockSpec(memory_space=pltpu.VMEM),
        scratch_shapes=[
            pltpu.VMEM((tiles, pairs * PACK_PITCH, 128), f32),
            pltpu.VMEM((tiles, pairs, 128, 128), half),
            pltpu.VMEM((tiles, pairs, 128, 128), half),
            pltpu.VMEM((tiles, pairs * ROW_PITCH, 128), f32),
            pltpu.VMEM((tiles, pairs * ROW_PITCH, 128), f32),
            pltpu.VMEM((tiles, pairs * ROW_PITCH, 128), f32),
            pltpu.VMEM((tiles, pairs * ROW_PITCH, 128), f32),
            pltpu.VMEM((tiles, pairs * ROW_PITCH, 128), f32),
            pltpu.VMEM((SIDE, SIDE), half),
            pltpu.VMEM((SHORT, SHORT), half),
            pltpu.VMEM((own, own), half),
            pltpu.VMEM((far, own), half),
            pltpu.VMEM((own, far), half),
            pltpu.VMEM((FLAT, elements), f32),
            pltpu.VMEM((FLAT, elements), f32),
            pltpu.VMEM((SIDE, own), f32),
            pltpu.VMEM((SIDE, own), half),
            pltpu.VMEM((SIDE, far), half),
            pltpu.VMEM((SIDE, own), half),
            pltpu.VMEM((ROUNDS, SIDE, 128), f32),
            pltpu.VMEM((4, ROUNDS, SIDE, 128), f32),
            pltpu.VMEM((count, 8, 128), f32),
            pltpu.VMEM((count, 8, 128), f32),
            pltpu.VMEM((count, 8, 128), f32),
            pltpu.VMEM((count, 8, 128), f32),
            pltpu.VMEM((16, 16), f32),
            pltpu.VMEM((MODES * MODES, owned), f32),
            pltpu.VMEM((owned, MODES * 128), f32),
            pltpu.VMEM((128, elements), f32),
            dma((4, ROUNDS, 2)),
            dma((4, ROUNDS, 2)),
            dma,
            dma,
            dma,
            dma,
        ],
        compiler_params=pltpu.CompilerParams(
            collective_id=0, has_side_effects=True, vmem_limit_bytes=58 * 2**20
        ),
    )(
        rhs.T,
        elem_block.transpose(1, 2, 0),
        block_inv.transpose(1, 2, 0),
        flux_jac,
        face_src.T,
        send_face,
        elem_route.reshape(1, elements),
        agg_local.T,
        coarse_block.transpose(1, 2, 0),
        coarse_inv.transpose(1, 2, 0),
        *const_tables(),
    )
    return result.T


def solution(mesh):
    return jax.shard_map(
        local,
        mesh=mesh,
        in_specs=(
            P(("dom", "sub"), None),
            P(("dom", "sub"), None, None),
            P(("dom", "sub"), None, None),
            P(),
            P(("dom", "sub"), None),
            P(("dom", "sub"), None),
            P(("dom", "sub")),
            P(("dom", "sub"), None),
            P(("dom", "sub"), None, None),
            P(("dom", "sub"), None, None),
        ),
        out_specs=P(("dom", "sub"), None),
        check_vma=False,
    )
```

```python
import functools
import math

import jax
import jax.numpy as jnp
import numpy as np
from jax import lax
from jax.experimental import pallas as pl
from jax.experimental.pallas import tpu as pltpu
from jax.sharding import PartitionSpec as P

COMPS = 13
NODES = 64
FACES = 6
FACE_NODES = 16
MODES = 4
ROUNDS = 5
MOST = 2
FLAT = COMPS * NODES
ROW_PITCH = 40
PACK_PITCH = 136
SIDE = COMPS * FACE_NODES
TRACE = FACES * SIDE

SHORT = 48
PENALTY = 0.5
MESH = pl.DeviceIdType.MESH


def node_tables():
    points = np.array([-1.0, -1.0 / math.sqrt(5.0), 1.0 / math.sqrt(5.0), 1.0])
    weights = np.array([1.0, 5.0, 5.0, 1.0]) / 6.0
    grid_i, grid_j, grid_k = np.meshgrid(points, points, points, indexing="ij")
    weight_grid = weights[:, None, None] * weights[None, :, None] * weights[None, None, :] / 8.0
    basis = np.stack([np.ones(64), grid_i.reshape(-1), grid_j.reshape(-1), grid_k.reshape(-1)])
    restrict = basis * weight_grid.reshape(-1)[None, :]
    number = np.arange(64).reshape(4, 4, 4)
    sides = [number[0], number[3], number[:, 0], number[:, 3], number[:, :, 0], number[:, :, 3]]
    face_index = np.stack([side.reshape(-1) for side in sides])
    return basis, restrict, face_index


def const_tables():
    basis, restrict, face_index = node_tables()
    eye = np.eye(COMPS)
    comp_row = np.pad(np.tile(np.repeat(eye, FACE_NODES, axis=0), (FACES, 1)), ((0, 0), (0, 3))).T
    node = np.eye(NODES)[face_index]
    row_node = np.broadcast_to(node[:, None], (FACES, COMPS, FACE_NODES, NODES)).reshape(TRACE, NODES)
    select = np.kron(np.eye(2), node.reshape(FACES * FACE_NODES, NODES))
    restrict_t = np.zeros((128, FLAT))
    restrict_t[: COMPS * MODES] = np.kron(eye, restrict)
    basis_t = np.zeros((FLAT, 128))
    basis_t[:, : COMPS * MODES] = np.kron(eye, basis.T)
    to_short = np.zeros((FACES * SHORT, 128))
    from_short = np.zeros((TRACE, SHORT))
    normal = (1, 1, 2, 2, 3, 3)
    tangent = ((2, 3), (2, 3), (1, 3), (1, 3), (1, 2), (1, 2))
    for f in range(FACES):
        for c in range(COMPS):
            row = f * SHORT + 3 * c
            to_short[row, c * MODES] = 1.0
            to_short[row, c * MODES + normal[f]] = -1.0 if f % 2 == 0 else 1.0
            to_short[row + 1, c * MODES + tangent[f][0]] = 1.0
            to_short[row + 2, c * MODES + tangent[f][1]] = 1.0
            rows = slice(f * SIDE + c * FACE_NODES, f * SIDE + (c + 1) * FACE_NODES)
            from_short[rows, 3 * c] = 1.0
            from_short[rows, 3 * c + 1] = basis[tangent[f][0], face_index[f]]
            from_short[rows, 3 * c + 2] = basis[tangent[f][1], face_index[f]]
    pick = np.zeros((128, MODES * 128))
    coef = np.zeros((16, MODES * 128))
    for k in range(MODES):
        for c in range(COMPS):
            for m in range(MODES):
                pick[c * MODES + k, k * 128 + c * MODES + m] = 1.0
                coef[m * MODES + k, k * 128 + c * MODES + m] = 1.0
    half = jnp.bfloat16
    return (
        jnp.asarray(comp_row, half),
        jnp.asarray(row_node.T, half),
        jnp.asarray(select, half),
        jnp.asarray(to_short, half),
        jnp.asarray(from_short, half),
        *parts_of(restrict_t),
        *parts_of(basis_t),
        jnp.asarray(pick, half),
        jnp.asarray(coef, half),
    )


def parts_of(table):
    table = np.asarray(table, np.float32)
    high = table.astype(jnp.bfloat16)
    return jnp.asarray(high), jnp.asarray((table - high.astype(np.float32)).astype(jnp.bfloat16))


def dot(a, b):
    return jnp.dot(a, b, preferred_element_type=jnp.float32)


def general(a, b, dims):
    return lax.dot_general(a, b, (dims, ((), ())), preferred_element_type=jnp.float32)


def split(value):
    high = value.astype(jnp.bfloat16)
    return high, (value - high.astype(jnp.float32)).astype(jnp.bfloat16)


def dot_ones(ones, value, dims=((1,), (0,))):
    high, low = split(value)
    return general(ones, high, dims) + general(ones, low, dims)


def dot_split(value, ones, dims):
    high, low = split(value)
    return general(high, ones, dims) + general(low, ones, dims)


def dot_parts(table, value):
    high, low = split(value)
    return dot(table[0], high) + (dot(table[0], low) + dot(table[1], high))


def kernel(
    count, subs,
    rhs, blocks_far, inverse, jac, face_src, send_face, route, agg_local, cblock, cinv,
    comp_row, node_row, select, to_short, from_short,
    restrict_high_far, restrict_low_far, basis_high_far, basis_low_far, pick, coef,
    out,
    blocks, restrict_high, restrict_low, basis_high, basis_low, fetch_sem,
    stage, block_w, inverse_w, rhs_lam, state, work, resid_lam, delta,
    lift_t, lift_short, restrict_flux_high, restrict_flux_low, pick_local, pick_remote, pick_send,
    lifted, around, near, table, landed, jump, jump_short, sending, arriving,
    bucket, incoming, reply, answer, jac_pad, flat_solve, solve_wide, around_modes,
    send_sem, recv_sem, give_sem, take_sem, back_sem, home_sem, known,
):
    elements = rhs.shape[1]
    tiles = elements // 128
    own = FACES * elements
    far = ROUNDS * 128
    me = lax.axis_index("dom") * subs + lax.axis_index("sub")

    def place(flat):
        return (flat // subs, flat % subs)

    def partner(k):
        bit = 1 << k
        return me + bit * (1 - 2 * ((me // bit) % 2))

    fetches = [
        pltpu.make_async_copy(source, target, fetch_sem.at[i])
        for i, (source, target) in enumerate(
            (
                (blocks_far, blocks),
                (restrict_high_far, restrict_high),
                (restrict_low_far, restrict_low),
                (basis_high_far, basis_high),
                (basis_low_far, basis_low),
            )
        )
    ]
    barrier = pltpu.get_barrier_semaphore()

    bits = count.bit_length() - 1
    for k in range(bits):
        pl.semaphore_signal(barrier, inc=1, device_id=place(partner(k)), device_id_type=MESH)
    for fetch in fetches:
        fetch.start()

    half_lanes = lax.broadcasted_iota(jnp.int32, (32, 128), 1) < NODES
    pairs = elements // 8

    def pack(source, target):
        def transpose(n, carry):
            rows = source[n].astype(jnp.float32)
            flat = jnp.concatenate([rows[:, :128], rows[:, 128:]], axis=0).T
            for y in range(2):
                even, odd = flat[y * 64 : y * 64 + 32], flat[y * 64 + 32 : y * 64 + 64]
                stage[y, pl.ds(n, pairs, stride=PACK_PITCH), :] = jnp.where(half_lanes, even, odd)
                stage[y, pl.ds(NODES + n, pairs, stride=PACK_PITCH), :] = jnp.where(half_lanes, odd, even)
            return carry

        lax.fori_loop(0, NODES, transpose, 0, unroll=8)

        def cast(j, carry):
            rows = pl.ds(pl.multiple_of(j * PACK_PITCH, 8), 128)
            for y in range(2):
                target[y, j] = stage[y, rows, :].astype(jnp.bfloat16)
            return carry

        lax.fori_loop(0, pairs, cast, 0, unroll=4)

    lane = lax.broadcasted_iota(jnp.int32, (NODES, 128), 1)
    odd_lane = (lane // 32) % 2 == 1

    def to_lam(source, target):
        for c in range(COMPS):
            rows = slice(c * NODES, (c + 1) * NODES)
            low, high = source[rows, :128], source[rows, 128:]
            flat = jnp.concatenate(
                [jnp.where(odd_lane, high, low), jnp.where(odd_lane, low, high)], axis=0
            ).T
            for y in range(2):
                for x in range(2):
                    start = y * 64 + x * 32
                    target[y, pl.ds(16 * x + c, pairs, stride=ROW_PITCH), :] = flat[start : start + 32]

    def from_lam(source, emit):
        for c in range(COMPS):
            flat = jnp.concatenate(
                [
                    source[y, pl.ds(16 * x + c, pairs, stride=ROW_PITCH), :]
                    for y in range(2)
                    for x in range(2)
                ],
                axis=0,
            ).T
            even, odd = flat[:NODES], flat[NODES:]
            rows = slice(c * NODES, (c + 1) * NODES)
            emit(rows, slice(0, 128), jnp.where(odd_lane, odd, even))
            emit(rows, slice(128, 256), jnp.where(odd_lane, even, odd))

    low_half = half_lanes[:16]
    blank = jnp.zeros((16, 128), jnp.float32)

    def apply_blocks(load, weights, emit):
        def body(g, carry):
            for y in range(2):
                parts = []
                for i in range(2):
                    row = pl.multiple_of((2 * g + i) * ROW_PITCH, 8)
                    even = load(y, pl.ds(row, 16))
                    odd = pltpu.roll(load(y, pl.ds(row + 16, 16)), NODES, 1)
                    parts += [
                        jnp.where(low_half, even, blank),
                        jnp.where(low_half, odd, blank),
                        jnp.where(low_half, blank, even),
                        jnp.where(low_half, blank, odd),
                    ]
                left = jnp.concatenate(parts, axis=0).astype(jnp.bfloat16)
                right = weights[y, pl.ds(2 * g, 2)].reshape(256, 128)
                both = lax.dot_general(
                    left, right, (((1,), (1,)), ((), ())), preferred_element_type=jnp.float32
                )
                for i in range(2):
                    row = pl.multiple_of((2 * g + i) * ROW_PITCH, 8)
                    value = both[64 * i : 64 * i + 64, 128 * i : 128 * i + 128]
                    emit(y, pl.ds(row, 16), jnp.where(low_half, value[:16], value[32:48]))
                    emit(y, pl.ds(row + 16, 16), jnp.where(low_half, value[48:], value[16:32]))
            return carry

        lax.fori_loop(0, pairs // 2, body, 0, unroll=8)

    def load_from(source):
        return lambda y, rows: source[y, rows, :]

    def store(target):
        def emit(y, rows, value):
            target[y, rows, :] = value
        return emit

    def add_to(target):
        def emit(y, rows, value):
            target[y, rows, :] = target[y, rows, :] + value
        return emit

    pack(inverse, inverse_w)
    to_lam(rhs, rhs_lam)
    apply_blocks(load_from(rhs_lam), inverse_w, store(state))

    def column(row):
        element = (row * 43691) >> 18
        return jnp.where(row < own, (row - element * FACES) * elements + element, row)

    def one_hot(rows, wanted, value=1.0):
        index = lax.broadcasted_iota(jnp.int32, (rows, wanted.shape[1]), 0)
        return jnp.where(index == wanted, value, 0.0).astype(jnp.bfloat16)

    for k in range(ROUNDS):
        wanted = column(send_face[k : k + 1, :])

        def send_rows(f, carry):
            rows = pl.ds(pl.multiple_of(f * elements, elements), elements)
            pick_send[rows, k * 128 : (k + 1) * 128] = one_hot(elements, wanted - f * elements)
            return carry

        lax.fori_loop(0, FACES, send_rows, 0)

    def local_tables():
        jac_pad[...] = jnp.zeros_like(jac_pad)
        jac_pad[:COMPS, :COMPS] = PENALTY * jac[...]
        spread_jac = general(jac_pad[...].astype(jnp.bfloat16), comp_row[...], ((0,), (0,)))
        for c in range(COMPS):
            lift_t[c * NODES : (c + 1) * NODES, :] = node_row[...] * spread_jac[
                c : c + 1, :
            ].astype(jnp.bfloat16)
        row = lax.broadcasted_iota(jnp.int32, (elements, elements), 0)
        mine = jnp.where(row == lax.broadcasted_iota(jnp.int32, (elements, elements), 1), 1.0, 0.0)
        for f in range(FACES):
            lanes = slice(f * elements, (f + 1) * elements)
            wanted = column(face_src[f : f + 1, :])

            def local_rows(g, carry):
                rows = pl.ds(pl.multiple_of(g * elements, elements), elements)
                pick_local[rows, lanes] = one_hot(elements, wanted - g * elements, -1.0)
                return carry

            lax.fori_loop(0, FACES, local_rows, 0)
            pick_local[lanes, lanes] = pick_local[lanes, lanes] + mine.astype(jnp.bfloat16)

            def remote_rows(k, carry):
                rows = pl.ds(pl.multiple_of(k * 128, 128), 128)
                pick_remote[rows, lanes] = one_hot(128, wanted - own - k * 128, -1.0)
                return carry

            lax.fori_loop(0, ROUNDS, remote_rows, 0)

    odd_face = (lax.broadcasted_iota(jnp.int32, (FACES * FACE_NODES, 128), 1) // 32) % 2 == 1

    def traces():
        for c in range(COMPS):
            flat = jnp.concatenate(
                [
                    state[y, pl.ds(16 * x + c, pairs, stride=ROW_PITCH), :]
                    for y in range(2)
                    for x in range(2)
                ],
                axis=0,
            ).astype(jnp.bfloat16)
            value = general(select[...], flat, ((1,), (1,)))
            even, odd = value[: FACES * FACE_NODES], value[FACES * FACE_NODES :]
            low = jnp.where(odd_face, odd, even).astype(jnp.bfloat16)
            high = jnp.where(odd_face, even, odd).astype(jnp.bfloat16)
            rows = slice(c * FACE_NODES, (c + 1) * FACE_NODES)
            for f in range(FACES):
                part = slice(f * FACE_NODES, (f + 1) * FACE_NODES)
                table[rows, f * elements : f * elements + 128] = low[part]
                table[rows, f * elements + 128 : (f + 1) * elements] = high[part]

    def begin(number, rows):
        copies = {}
        for group in ((4, 3), (2, 1, 0)):
            lanes = slice(min(group) * 128, (max(group) + 1) * 128)
            outgoing = dot(table[:rows, :], pick_send[:, lanes])
            for k in group:
                start = (k - min(group)) * 128
                sending[k, :rows, :] = outgoing[:, start : start + 128]
                copies[k] = pltpu.make_async_remote_copy(
                    src_ref=sending.at[k, pl.ds(0, rows)],
                    dst_ref=arriving.at[number, k, pl.ds(0, rows)],
                    send_sem=send_sem.at[number, k],
                    recv_sem=recv_sem.at[number, k],
                    device_id=place(partner(k)),
                    device_id_type=MESH,
                )
                copies[k].start()
        return copies

    def end(number, rows, copies, target):
        def land(k):
            copies[k].wait_recv()
            landed[:rows, k * 128 : (k + 1) * 128] = arriving[number, k, :rows, :].astype(
                jnp.bfloat16
            )

        for k in (0, 1, 2):
            land(k)
        near[:rows, :] = near[:rows, :] + dot(landed[:rows, : 3 * 128], pick_remote[: 3 * 128, :])
        for k in (3, 4):
            land(k)
        value = near[:rows, :] + dot(landed[:rows, 3 * 128 :], pick_remote[3 * 128 :, :])
        for f in range(FACES):
            target[f * rows : (f + 1) * rows, :] = value[:, f * elements : (f + 1) * elements].astype(
                jnp.bfloat16
            )
        for k in range(ROUNDS):
            copies[k].wait_send()

    def operate(number, between=None, beside=None):
        traces()
        copies = begin(number, SIDE)
        if between is not None:
            between()
        near[...] = dot(table[...], pick_local[...])
        apply_blocks(load_from(state), block_w, store(work))
        if beside is not None:
            beside()
        end(number, SIDE, copies, jump)

    def residual(y, rows):
        return rhs_lam[y, rows, :] - work[y, rows, :] - delta[y, rows, :]

    def sweep(number, between=None):
        operate(number, between)
        lifted[...] = dot(lift_t[...], jump[...])
        to_lam(lifted, delta)
        apply_blocks(residual, inverse_w, add_to(state))

    def exchange(source, target, sent, got, between=None):
        def copy_of(step):
            other = (me + step) % count
            return pltpu.make_async_remote_copy(
                src_ref=source.at[other, pl.ds(0, MOST)],
                dst_ref=target.at[me, pl.ds(0, MOST)],
                send_sem=sent,
                recv_sem=got,
                device_id=place(other),
                device_id_type=MESH,
            )

        def start(step, carry):
            copy_of(step).start()
            return carry

        lax.fori_loop(1, count, start, 0, unroll=4)
        target[me] = source[me]
        if between is not None:
            between()
        everything = pl.ds(0, count - 1), pl.ds(0, MOST)
        for semaphore in (got, sent):
            pltpu.make_async_copy(source.at[everything], target.at[everything], semaphore).wait()

    told = []

    def tell():
        if told:
            pl.semaphore_wait(known.at[told[-1]], 1)
        if len(told) < bits:
            k = len(told)
            pl.semaphore_signal(
                known.at[k], inc=1, device_id=place(partner(k)), device_id_type=MESH
            )
            told.append(k)

    def behind_first():
        tell()
        local_tables()
        tell()
        for fetch in fetches:
            fetch.wait()
        pack(blocks, block_w)
        tell()

    owned = cblock.shape[2]
    inverse_rows = [cinv[m] for m in range(MODES)]
    block_rows = [cblock[m] for m in range(MODES)]

    def times(rows, k, other):
        return rows[k : k + 1, :] * other

    def solve_rows():
        inner = [
            sum(times(block_rows[p], q, inverse_rows[q]) for q in range(MODES)) for p in range(MODES)
        ]
        for m in range(MODES):
            flat_solve[m * MODES : (m + 1) * MODES, :] = 2.0 * inverse_rows[m] - sum(
                times(inverse_rows[m], p, inner[p]) for p in range(MODES)
            )

    solve_rows()
    pl.semaphore_wait(barrier, bits)
    sweep(0, behind_first)

    def behind_second():
        tell()

        def emit_around(rows, lanes, value):
            around[rows, lanes] = rhs[rows, lanes] - value

        from_lam(work, emit_around)
        around_modes[...] = dot_parts((restrict_high[...], restrict_low[...]), around[...])
        for f in range(FACES):
            rows = slice(f * SIDE, (f + 1) * SIDE)
            lift_short[:, f * SHORT : (f + 1) * SHORT] = dot(
                lift_t[:, rows], from_short[rows, :]
            ).astype(jnp.bfloat16)
        high, low = split(
            dot(restrict_high[...], lift_t[...]) + dot(restrict_low[...], lift_t[...])
        )
        restrict_flux_high[...] = high
        restrict_flux_low[...] = low
        solve_wide[...] = dot_split(flat_solve[...], coef[...], ((0,), (0,)))

    operate(1, between=tell, beside=behind_second)
    while len(told) < bits:
        tell()
    tell()
    partial = around_modes[...] - (
        dot(restrict_flux_high[...], jump[...]) + dot(restrict_flux_low[...], jump[...])
    )
    route_row = (route[...] // MOST) * 8 + route[...] % MOST
    to_bucket = one_hot(count * 8, route_row)
    bucket[...] = dot_ones(to_bucket, partial, ((1,), (1,))).reshape(count, 8, 128)

    def behind_bucket():
        lifted[...] = dot(lift_t[...], jump[...])
        to_lam(lifted, delta)
        resid_lam[...] = rhs_lam[...] - work[...] - delta[...]

    exchange(bucket, incoming, give_sem, take_sem, behind_bucket)
    members = [one_hot(owned, agg_local[s : s + 1, :]) for s in range(MOST)]
    coarse_rhs = sum(dot_ones(members[s], incoming[:, s, :]) for s in range(MOST))
    product = solve_wide[...] * dot_split(coarse_rhs, pick[...], ((1,), (0,)))
    solved = product[:, :128] + product[:, 128:256] + product[:, 256:384] + product[:, 384:]
    reply[...] = jnp.zeros_like(reply)
    for s in range(MOST):
        reply[:, s, :] = dot_ones(members[s], solved, ((0,), (0,)))
    exchange(reply, answer, back_sem, home_sem)
    slot = lax.broadcasted_iota(jnp.int32, (count * 8, 128), 0) % 8
    returned = jnp.where(slot < MOST, answer[...].reshape(count * 8, 128), 0.0)
    correction = dot_split(returned, to_bucket, ((0,), (0,)))

    short = dot_ones(to_short[...], correction).astype(jnp.bfloat16)
    for f in range(FACES):
        table[:SHORT, f * elements : (f + 1) * elements] = short[f * SHORT : (f + 1) * SHORT]
    copies = begin(2, SHORT)
    lifted[...] = dot_parts((basis_high[...], basis_low[...]), correction)
    to_lam(lifted, delta)
    state[...] = state[...] + delta[...]
    apply_blocks(load_from(delta), block_w, store(work))
    resid_lam[...] = resid_lam[...] - work[...]
    near[:SHORT, :] = dot(table[:SHORT, :], pick_local[...])
    end(2, SHORT, copies, jump_short)
    lifted[...] = dot(lift_short[...], jump_short[...])
    to_lam(lifted, delta)

    def coarse_residual(y, rows):
        return resid_lam[y, rows, :] - delta[y, rows, :]

    apply_blocks(coarse_residual, inverse_w, add_to(state))
    sweep(3)

    def emit_out(rows, lanes, value):
        out[rows, lanes] = value

    from_lam(state, emit_out)


def local(
    rhs,
    elem_block,
    block_inv,
    flux_jac,
    face_src,
    send_face,
    elem_route,
    agg_local,
    coarse_block,
    coarse_inv,
):
    elements = rhs.shape[0]
    count = lax.axis_size(("dom", "sub"))
    subs = lax.axis_size("sub")
    owned = coarse_block.shape[0]
    tiles = elements // 128
    pairs = elements // 8
    own = FACES * elements
    far = ROUNDS * 128
    f32, half = jnp.float32, jnp.bfloat16
    dma = pltpu.SemaphoreType.DMA
    near_spec = pl.BlockSpec(memory_space=pltpu.VMEM)
    far_spec = pl.BlockSpec(memory_space=pl.ANY)
    result = pl.pallas_call(
        functools.partial(kernel, count, subs),
        out_shape=jax.ShapeDtypeStruct((FLAT, elements), f32),
        in_specs=[near_spec, far_spec] + [near_spec] * 13 + [far_spec] * 4 + [near_spec] * 2,
        out_specs=pl.BlockSpec(memory_space=pltpu.VMEM),
        scratch_shapes=[
            pltpu.VMEM((NODES, NODES, elements), half),
            pltpu.VMEM((128, FLAT), half),
            pltpu.VMEM((128, FLAT), half),
            pltpu.VMEM((FLAT, 128), half),
            pltpu.VMEM((FLAT, 128), half),
            dma((5,)),
            pltpu.VMEM((tiles, pairs * PACK_PITCH, 128), f32),
            pltpu.VMEM((tiles, pairs, 128, 128), half),
            pltpu.VMEM((tiles, pairs, 128, 128), half),
            pltpu.VMEM((tiles, pairs * ROW_PITCH, 128), f32),
            pltpu.VMEM((tiles, pairs * ROW_PITCH, 128), f32),
            pltpu.VMEM((tiles, pairs * ROW_PITCH, 128), f32),
            pltpu.VMEM((tiles, pairs * ROW_PITCH, 128), f32),
            pltpu.VMEM((tiles, pairs * ROW_PITCH, 128), f32),
            pltpu.VMEM((FLAT, TRACE), half),
            pltpu.VMEM((FLAT, FACES * SHORT), half),
            pltpu.VMEM((128, TRACE), half),
            pltpu.VMEM((128, TRACE), half),
            pltpu.VMEM((own, own), half),
            pltpu.VMEM((far, own), half),
            pltpu.VMEM((own, far), half),
            pltpu.VMEM((FLAT, elements), f32),
            pltpu.VMEM((FLAT, elements), f32),
            pltpu.VMEM((SIDE, own), f32),
            pltpu.VMEM((SIDE, own), half),
            pltpu.VMEM((SIDE, far), half),
            pltpu.VMEM((TRACE, elements), half),
            pltpu.VMEM((FACES * SHORT, elements), half),
            pltpu.VMEM((ROUNDS, SIDE, 128), f32),
            pltpu.VMEM((4, ROUNDS, SIDE, 128), f32),
            pltpu.VMEM((count, 8, 128), f32),
            pltpu.VMEM((count, 8, 128), f32),
            pltpu.VMEM((count, 8, 128), f32),
            pltpu.VMEM((count, 8, 128), f32),
            pltpu.VMEM((16, 16), f32),
            pltpu.VMEM((MODES * MODES, owned), f32),
            pltpu.VMEM((owned, MODES * 128), f32),
            pltpu.VMEM((128, elements), f32),
            dma((4, ROUNDS)),
            dma((4, ROUNDS)),
            dma,
            dma,
            dma,
            dma,
            pltpu.SemaphoreType.REGULAR((count.bit_length() - 1,)),
        ],
        compiler_params=pltpu.CompilerParams(
            collective_id=0, has_side_effects=True, vmem_limit_bytes=58 * 2**20
        ),
    )(
        rhs.T,
        elem_block.transpose(1, 2, 0),
        block_inv.transpose(1, 2, 0),
        flux_jac,
        face_src.T,
        send_face,
        elem_route.reshape(1, elements),
        agg_local.T,
        coarse_block.transpose(1, 2, 0),
        coarse_inv.transpose(1, 2, 0),
        *const_tables(),
    )
    return result.T


def solution(mesh):
    return jax.shard_map(
        local,
        mesh=mesh,
        in_specs=(
            P(("dom", "sub"), None),
            P(("dom", "sub"), None, None),
            P(("dom", "sub"), None, None),
            P(),
            P(("dom", "sub"), None),
            P(("dom", "sub"), None),
            P(("dom", "sub")),
            P(("dom", "sub"), None),
            P(("dom", "sub"), None, None),
            P(("dom", "sub"), None, None),
        ),
        out_specs=P(("dom", "sub"), None),
        check_vma=False,
    )
```

```python
import functools
import math

import jax
import jax.numpy as jnp
import numpy as np
from jax import lax
from jax.experimental import pallas as pl
from jax.experimental.pallas import tpu as pltpu
from jax.sharding import PartitionSpec as P

COMPS = 13
NODES = 64
FACES = 6
FACE_NODES = 16
MODES = 4
ROUNDS = 5
MOST = 2
FLAT = COMPS * NODES
ROW_PITCH = 40
PACK_PITCH = 136
SIDE = COMPS * FACE_NODES
TRACE = FACES * SIDE

SHORT = 48
PENALTY = 0.5
MESH = pl.DeviceIdType.MESH


def node_tables():
    points = np.array([-1.0, -1.0 / math.sqrt(5.0), 1.0 / math.sqrt(5.0), 1.0])
    weights = np.array([1.0, 5.0, 5.0, 1.0]) / 6.0
    grid_i, grid_j, grid_k = np.meshgrid(points, points, points, indexing="ij")
    weight_grid = weights[:, None, None] * weights[None, :, None] * weights[None, None, :] / 8.0
    basis = np.stack([np.ones(64), grid_i.reshape(-1), grid_j.reshape(-1), grid_k.reshape(-1)])
    restrict = basis * weight_grid.reshape(-1)[None, :]
    number = np.arange(64).reshape(4, 4, 4)
    sides = [number[0], number[3], number[:, 0], number[:, 3], number[:, :, 0], number[:, :, 3]]
    face_index = np.stack([side.reshape(-1) for side in sides])
    return basis, restrict, face_index


def const_tables():
    basis, restrict, face_index = node_tables()
    eye = np.eye(COMPS)
    comp_row = np.pad(np.tile(np.repeat(eye, FACE_NODES, axis=0), (FACES, 1)), ((0, 0), (0, 3))).T
    node = np.eye(NODES)[face_index]
    row_node = np.broadcast_to(node[:, None], (FACES, COMPS, FACE_NODES, NODES)).reshape(TRACE, NODES)
    select = np.kron(np.eye(2), node.reshape(FACES * FACE_NODES, NODES))
    restrict_t = np.zeros((128, FLAT))
    restrict_t[: COMPS * MODES] = np.kron(eye, restrict)
    basis_t = np.zeros((FLAT, 128))
    basis_t[:, : COMPS * MODES] = np.kron(eye, basis.T)
    to_short = np.zeros((FACES * SHORT, 128))
    from_short = np.zeros((TRACE, SHORT))
    normal = (1, 1, 2, 2, 3, 3)
    tangent = ((2, 3), (2, 3), (1, 3), (1, 3), (1, 2), (1, 2))
    for f in range(FACES):
        for c in range(COMPS):
            row = f * SHORT + 3 * c
            to_short[row, c * MODES] = 1.0
            to_short[row, c * MODES + normal[f]] = -1.0 if f % 2 == 0 else 1.0
            to_short[row + 1, c * MODES + tangent[f][0]] = 1.0
            to_short[row + 2, c * MODES + tangent[f][1]] = 1.0
            rows = slice(f * SIDE + c * FACE_NODES, f * SIDE + (c + 1) * FACE_NODES)
            from_short[rows, 3 * c] = 1.0
            from_short[rows, 3 * c + 1] = basis[tangent[f][0], face_index[f]]
            from_short[rows, 3 * c + 2] = basis[tangent[f][1], face_index[f]]
    pick = np.zeros((128, MODES * 128))
    coef = np.zeros((16, MODES * 128))
    for k in range(MODES):
        for c in range(COMPS):
            for m in range(MODES):
                pick[c * MODES + k, k * 128 + c * MODES + m] = 1.0
                coef[m * MODES + k, k * 128 + c * MODES + m] = 1.0
    half = jnp.bfloat16
    return (
        jnp.asarray(comp_row, half),
        jnp.asarray(row_node.T, half),
        jnp.asarray(select, half),
        jnp.asarray(to_short, half),
        jnp.asarray(from_short, half),
        *parts_of(restrict_t),
        *parts_of(basis_t),
        jnp.asarray(pick, half),
        jnp.asarray(coef, half),
    )


def parts_of(table):
    table = np.asarray(table, np.float32)
    high = table.astype(jnp.bfloat16)
    return jnp.asarray(high), jnp.asarray((table - high.astype(np.float32)).astype(jnp.bfloat16))


def dot(a, b):
    return jnp.dot(a, b, preferred_element_type=jnp.float32)


def general(a, b, dims):
    return lax.dot_general(a, b, (dims, ((), ())), preferred_element_type=jnp.float32)


def split(value):
    high = value.astype(jnp.bfloat16)
    return high, (value - high.astype(jnp.float32)).astype(jnp.bfloat16)


def dot_ones(ones, value, dims=((1,), (0,))):
    high, low = split(value)
    return general(ones, high, dims) + general(ones, low, dims)


def dot_split(value, ones, dims):
    high, low = split(value)
    return general(high, ones, dims) + general(low, ones, dims)


def dot_parts(table, value):
    high, low = split(value)
    return dot(table[0], high) + (dot(table[0], low) + dot(table[1], high))


def kernel(
    count, subs,
    rhs, blocks_far, inverse_far, jac, face_src, send_face, route, agg_local, cblock, cinv,
    comp_row, node_row, select, to_short, from_short,
    restrict_high_far, restrict_low_far, basis_high_far, basis_low_far, pick, coef,
    out,
    blocks, inverse, restrict_high, restrict_low, basis_high, basis_low, fetch_sem,
    stage, block_w, inverse_w, rhs_lam, state, work, resid_lam, delta,
    lift_t, lift_short, restrict_flux_high, restrict_flux_low, pick_local, pick_remote, pick_send,
    lifted, around, near, table, landed, jump, jump_short, sending, arriving,
    bucket, incoming, reply, answer, jac_pad, flat_solve, solve_wide, around_modes,
    send_sem, recv_sem, give_sem, take_sem, back_sem, home_sem, known,
):
    elements = rhs.shape[1]
    tiles = elements // 128
    own = FACES * elements
    far = ROUNDS * 128
    me = lax.axis_index("dom") * subs + lax.axis_index("sub")

    def place(flat):
        return (flat // subs, flat % subs)

    def partner(k):
        bit = 1 << k
        return me + bit * (1 - 2 * ((me // bit) % 2))

    slabs = [
        pltpu.make_async_copy(
            inverse_far.at[pl.ds(i * 16, 16)], inverse.at[pl.ds(i * 16, 16)], fetch_sem.at[5 + i]
        )
        for i in range(4)
    ]
    for slab in slabs:
        slab.start()
    fetches = [
        pltpu.make_async_copy(source, target, fetch_sem.at[i])
        for i, (source, target) in enumerate(
            (
                (blocks_far, blocks),
                (restrict_high_far, restrict_high),
                (restrict_low_far, restrict_low),
                (basis_high_far, basis_high),
                (basis_low_far, basis_low),
            )
        )
    ]
    barrier = pltpu.get_barrier_semaphore()

    bits = count.bit_length() - 1
    for k in range(bits):
        pl.semaphore_signal(barrier, inc=1, device_id=place(partner(k)), device_id_type=MESH)
    for fetch in fetches:
        fetch.start()

    half_lanes = lax.broadcasted_iota(jnp.int32, (32, 128), 1) < NODES
    pairs = elements // 8

    def pack(source, target, arrivals=()):
        def transpose(n, carry):
            rows = source[n].astype(jnp.float32)
            flat = jnp.concatenate([rows[:, :128], rows[:, 128:]], axis=0).T
            for y in range(2):
                even, odd = flat[y * 64 : y * 64 + 32], flat[y * 64 + 32 : y * 64 + 64]
                stage[y, pl.ds(n, pairs, stride=PACK_PITCH), :] = jnp.where(half_lanes, even, odd)
                stage[y, pl.ds(NODES + n, pairs, stride=PACK_PITCH), :] = jnp.where(half_lanes, odd, even)
            return carry

        for i in range(4):
            if arrivals:
                arrivals[i].wait()
            lax.fori_loop(i * 16, i * 16 + 16, transpose, 0, unroll=8)

        def cast(j, carry):
            rows = pl.ds(pl.multiple_of(j * PACK_PITCH, 8), 128)
            for y in range(2):
                target[y, j] = stage[y, rows, :].astype(jnp.bfloat16)
            return carry

        lax.fori_loop(0, pairs, cast, 0, unroll=4)

    lane = lax.broadcasted_iota(jnp.int32, (NODES, 128), 1)
    odd_lane = (lane // 32) % 2 == 1

    def to_lam(source, target):
        for c in range(COMPS):
            rows = slice(c * NODES, (c + 1) * NODES)
            low, high = source[rows, :128], source[rows, 128:]
            flat = jnp.concatenate(
                [jnp.where(odd_lane, high, low), jnp.where(odd_lane, low, high)], axis=0
            ).T
            for y in range(2):
                for x in range(2):
                    start = y * 64 + x * 32
                    target[y, pl.ds(16 * x + c, pairs, stride=ROW_PITCH), :] = flat[start : start + 32]

    def from_lam(source, emit):
        for c in range(COMPS):
            flat = jnp.concatenate(
                [
                    source[y, pl.ds(16 * x + c, pairs, stride=ROW_PITCH), :]
                    for y in range(2)
                    for x in range(2)
                ],
                axis=0,
            ).T
            even, odd = flat[:NODES], flat[NODES:]
            rows = slice(c * NODES, (c + 1) * NODES)
            emit(rows, slice(0, 128), jnp.where(odd_lane, odd, even))
            emit(rows, slice(128, 256), jnp.where(odd_lane, even, odd))

    low_half = half_lanes[:16]
    blank = jnp.zeros((16, 128), jnp.float32)

    def apply_blocks(load, weights, emit):
        def body(g, carry):
            for y in range(2):
                parts = []
                for i in range(2):
                    row = pl.multiple_of((2 * g + i) * ROW_PITCH, 8)
                    even = load(y, pl.ds(row, 16))
                    odd = pltpu.roll(load(y, pl.ds(row + 16, 16)), NODES, 1)
                    parts += [
                        jnp.where(low_half, even, blank),
                        jnp.where(low_half, odd, blank),
                        jnp.where(low_half, blank, even),
                        jnp.where(low_half, blank, odd),
                    ]
                left = jnp.concatenate(parts, axis=0).astype(jnp.bfloat16)
                right = weights[y, pl.ds(2 * g, 2)].reshape(256, 128)
                both = lax.dot_general(
                    left, right, (((1,), (1,)), ((), ())), preferred_element_type=jnp.float32
                )
                for i in range(2):
                    row = pl.multiple_of((2 * g + i) * ROW_PITCH, 8)
                    value = both[64 * i : 64 * i + 64, 128 * i : 128 * i + 128]
                    emit(y, pl.ds(row, 16), jnp.where(low_half, value[:16], value[32:48]))
                    emit(y, pl.ds(row + 16, 16), jnp.where(low_half, value[48:], value[16:32]))
            return carry

        lax.fori_loop(0, pairs // 2, body, 0, unroll=8)

    def load_from(source):
        return lambda y, rows: source[y, rows, :]

    def store(target):
        def emit(y, rows, value):
            target[y, rows, :] = value
        return emit

    def add_to(target):
        def emit(y, rows, value):
            target[y, rows, :] = target[y, rows, :] + value
        return emit

    def column(row):
        element = (row * 43691) >> 18
        return jnp.where(row < own, (row - element * FACES) * elements + element, row)

    def one_hot(rows, wanted, value=1.0):
        index = lax.broadcasted_iota(jnp.int32, (rows, wanted.shape[1]), 0)
        return jnp.where(index == wanted, value, 0.0).astype(jnp.bfloat16)

    for k in range(ROUNDS):
        wanted = column(send_face[k : k + 1, :])

        def send_rows(f, carry):
            rows = pl.ds(pl.multiple_of(f * elements, elements), elements)
            pick_send[rows, k * 128 : (k + 1) * 128] = one_hot(elements, wanted - f * elements)
            return carry

        lax.fori_loop(0, FACES, send_rows, 0)

    to_lam(rhs, rhs_lam)
    pack(inverse, inverse_w, slabs)
    apply_blocks(load_from(rhs_lam), inverse_w, store(state))

    def local_tables():
        jac_pad[...] = jnp.zeros_like(jac_pad)
        jac_pad[:COMPS, :COMPS] = PENALTY * jac[...]
        spread_jac = general(jac_pad[...].astype(jnp.bfloat16), comp_row[...], ((0,), (0,)))
        for c in range(COMPS):
            lift_t[c * NODES : (c + 1) * NODES, :] = node_row[...] * spread_jac[
                c : c + 1, :
            ].astype(jnp.bfloat16)
        row = lax.broadcasted_iota(jnp.int32, (elements, elements), 0)
        mine = jnp.where(row == lax.broadcasted_iota(jnp.int32, (elements, elements), 1), 1.0, 0.0)
        for f in range(FACES):
            lanes = slice(f * elements, (f + 1) * elements)
            wanted = column(face_src[f : f + 1, :])

            def local_rows(g, carry):
                rows = pl.ds(pl.multiple_of(g * elements, elements), elements)
                pick_local[rows, lanes] = one_hot(elements, wanted - g * elements, -1.0)
                return carry

            lax.fori_loop(0, FACES, local_rows, 0)
            pick_local[lanes, lanes] = pick_local[lanes, lanes] + mine.astype(jnp.bfloat16)

            def remote_rows(k, carry):
                rows = pl.ds(pl.multiple_of(k * 128, 128), 128)
                pick_remote[rows, lanes] = one_hot(128, wanted - own - k * 128, -1.0)
                return carry

            lax.fori_loop(0, ROUNDS, remote_rows, 0)

    odd_face = (lax.broadcasted_iota(jnp.int32, (FACES * FACE_NODES, 128), 1) // 32) % 2 == 1

    def traces():
        for c in range(COMPS):
            flat = jnp.concatenate(
                [
                    state[y, pl.ds(16 * x + c, pairs, stride=ROW_PITCH), :]
                    for y in range(2)
                    for x in range(2)
                ],
                axis=0,
            ).astype(jnp.bfloat16)
            value = general(select[...], flat, ((1,), (1,)))
            even, odd = value[: FACES * FACE_NODES], value[FACES * FACE_NODES :]
            low = jnp.where(odd_face, odd, even).astype(jnp.bfloat16)
            high = jnp.where(odd_face, even, odd).astype(jnp.bfloat16)
            rows = slice(c * FACE_NODES, (c + 1) * FACE_NODES)
            for f in range(FACES):
                part = slice(f * FACE_NODES, (f + 1) * FACE_NODES)
                table[rows, f * elements : f * elements + 128] = low[part]
                table[rows, f * elements + 128 : (f + 1) * elements] = high[part]

    def begin(number, rows):
        copies = {}
        for group in ((4,), (3,), (2, 1, 0)):
            lanes = slice(min(group) * 128, (max(group) + 1) * 128)
            outgoing = dot(table[:rows, :], pick_send[:, lanes])
            for k in group:
                start = (k - min(group)) * 128
                sending[k, :rows, :] = outgoing[:, start : start + 128]
                copies[k] = pltpu.make_async_remote_copy(
                    src_ref=sending.at[k, pl.ds(0, rows)],
                    dst_ref=arriving.at[number, k, pl.ds(0, rows)],
                    send_sem=send_sem.at[number, k],
                    recv_sem=recv_sem.at[number, k],
                    device_id=place(partner(k)),
                    device_id_type=MESH,
                )
                copies[k].start()
        return copies

    def end(number, rows, copies, target):
        def land(k):
            copies[k].wait_recv()
            landed[:rows, k * 128 : (k + 1) * 128] = arriving[number, k, :rows, :].astype(
                jnp.bfloat16
            )

        for k in (0, 1, 2):
            land(k)
        near[:rows, :] = near[:rows, :] + dot(landed[:rows, : 3 * 128], pick_remote[: 3 * 128, :])
        for k in (3, 4):
            land(k)
        value = near[:rows, :] + dot(landed[:rows, 3 * 128 :], pick_remote[3 * 128 :, :])
        for f in range(FACES):
            target[f * rows : (f + 1) * rows, :] = value[:, f * elements : (f + 1) * elements].astype(
                jnp.bfloat16
            )
        for k in range(ROUNDS):
            copies[k].wait_send()

    def operate(number, between=None, beside=None):
        traces()
        copies = begin(number, SIDE)
        if between is not None:
            between()
        near[...] = dot(table[...], pick_local[...])
        apply_blocks(load_from(state), block_w, store(work))
        if beside is not None:
            beside()
        end(number, SIDE, copies, jump)

    def residual(y, rows):
        return rhs_lam[y, rows, :] - work[y, rows, :] - delta[y, rows, :]

    def sweep(number, between=None):
        operate(number, between)
        lifted[...] = dot(lift_t[...], jump[...])
        to_lam(lifted, delta)
        apply_blocks(residual, inverse_w, add_to(state))

    def exchange(source, target, sent, got, between=None):
        def copy_of(step):
            other = (me + step) % count
            return pltpu.make_async_remote_copy(
                src_ref=source.at[other, pl.ds(0, MOST)],
                dst_ref=target.at[me, pl.ds(0, MOST)],
                send_sem=sent,
                recv_sem=got,
                device_id=place(other),
                device_id_type=MESH,
            )

        def start(step, carry):
            copy_of(step).start()
            return carry

        lax.fori_loop(1, count, start, 0, unroll=4)
        target[me] = source[me]
        if between is not None:
            between()
        everything = pl.ds(0, count - 1), pl.ds(0, MOST)
        for semaphore in (got, sent):
            pltpu.make_async_copy(source.at[everything], target.at[everything], semaphore).wait()

    told = []

    def tell():
        if told:
            pl.semaphore_wait(known.at[told[-1]], 1)
        if len(told) < bits:
            k = len(told)
            pl.semaphore_signal(
                known.at[k], inc=1, device_id=place(partner(k)), device_id_type=MESH
            )
            told.append(k)

    def behind_first():
        tell()
        local_tables()
        tell()
        for fetch in fetches:
            fetch.wait()
        pack(blocks, block_w)
        tell()

    owned = cblock.shape[2]
    inverse_rows = [cinv[m] for m in range(MODES)]
    block_rows = [cblock[m] for m in range(MODES)]

    def times(rows, k, other):
        return rows[k : k + 1, :] * other

    def solve_rows():
        inner = [
            sum(times(block_rows[p], q, inverse_rows[q]) for q in range(MODES)) for p in range(MODES)
        ]
        for m in range(MODES):
            flat_solve[m * MODES : (m + 1) * MODES, :] = 2.0 * inverse_rows[m] - sum(
                times(inverse_rows[m], p, inner[p]) for p in range(MODES)
            )

    solve_rows()
    pl.semaphore_wait(barrier, bits)
    sweep(0, behind_first)

    def behind_second():
        tell()

        def emit_around(rows, lanes, value):
            around[rows, lanes] = rhs[rows, lanes] - value

        from_lam(work, emit_around)
        around_modes[...] = dot_parts((restrict_high[...], restrict_low[...]), around[...])
        for f in range(FACES):
            rows = slice(f * SIDE, (f + 1) * SIDE)
            lift_short[:, f * SHORT : (f + 1) * SHORT] = dot(
                lift_t[:, rows], from_short[rows, :]
            ).astype(jnp.bfloat16)
        high, low = split(
            dot(restrict_high[...], lift_t[...]) + dot(restrict_low[...], lift_t[...])
        )
        restrict_flux_high[...] = high
        restrict_flux_low[...] = low
        solve_wide[...] = dot_split(flat_solve[...], coef[...], ((0,), (0,)))

    operate(1, between=tell, beside=behind_second)
    while len(told) < bits:
        tell()
    tell()
    partial = around_modes[...] - (
        dot(restrict_flux_high[...], jump[...]) + dot(restrict_flux_low[...], jump[...])
    )
    route_row = (route[...] // MOST) * 8 + route[...] % MOST
    to_bucket = one_hot(count * 8, route_row)
    bucket[...] = dot_ones(to_bucket, partial, ((1,), (1,))).reshape(count, 8, 128)

    def behind_bucket():
        lifted[...] = dot(lift_t[...], jump[...])
        to_lam(lifted, delta)
        resid_lam[...] = rhs_lam[...] - work[...] - delta[...]

    exchange(bucket, incoming, give_sem, take_sem, behind_bucket)
    members = [one_hot(owned, agg_local[s : s + 1, :]) for s in range(MOST)]
    coarse_rhs = sum(dot_ones(members[s], incoming[:, s, :]) for s in range(MOST))
    product = solve_wide[...] * dot_split(coarse_rhs, pick[...], ((1,), (0,)))
    solved = product[:, :128] + product[:, 128:256] + product[:, 256:384] + product[:, 384:]
    reply[...] = jnp.zeros_like(reply)
    for s in range(MOST):
        reply[:, s, :] = dot_ones(members[s], solved, ((0,), (0,)))
    exchange(reply, answer, back_sem, home_sem)
    slot = lax.broadcasted_iota(jnp.int32, (count * 8, 128), 0) % 8
    returned = jnp.where(slot < MOST, answer[...].reshape(count * 8, 128), 0.0)
    correction = dot_split(returned, to_bucket, ((0,), (0,)))

    short = dot_ones(to_short[...], correction).astype(jnp.bfloat16)
    for f in range(FACES):
        table[:SHORT, f * elements : (f + 1) * elements] = short[f * SHORT : (f + 1) * SHORT]
    copies = begin(2, SHORT)
    lifted[...] = dot_parts((basis_high[...], basis_low[...]), correction)
    to_lam(lifted, delta)
    state[...] = state[...] + delta[...]

    def take_from_residual(y, rows, value):
        resid_lam[y, rows, :] = resid_lam[y, rows, :] - value

    apply_blocks(load_from(delta), block_w, take_from_residual)
    near[:SHORT, :] = dot(table[:SHORT, :], pick_local[...])
    end(2, SHORT, copies, jump_short)
    lifted[...] = dot(lift_short[...], jump_short[...])
    to_lam(lifted, delta)

    def coarse_residual(y, rows):
        return resid_lam[y, rows, :] - delta[y, rows, :]

    apply_blocks(coarse_residual, inverse_w, add_to(state))
    sweep(3)

    def emit_out(rows, lanes, value):
        out[rows, lanes] = value

    from_lam(state, emit_out)


def local(
    rhs,
    elem_block,
    block_inv,
    flux_jac,
    face_src,
    send_face,
    elem_route,
    agg_local,
    coarse_block,
    coarse_inv,
):
    elements = rhs.shape[0]
    count = lax.axis_size(("dom", "sub"))
    subs = lax.axis_size("sub")
    owned = coarse_block.shape[0]
    tiles = elements // 128
    pairs = elements // 8
    own = FACES * elements
    far = ROUNDS * 128
    f32, half = jnp.float32, jnp.bfloat16
    dma = pltpu.SemaphoreType.DMA
    near_spec = pl.BlockSpec(memory_space=pltpu.VMEM)
    far_spec = pl.BlockSpec(memory_space=pl.ANY)
    result = pl.pallas_call(
        functools.partial(kernel, count, subs),
        out_shape=jax.ShapeDtypeStruct((FLAT, elements), f32),
        in_specs=[near_spec, far_spec, far_spec] + [near_spec] * 12 + [far_spec] * 4 + [near_spec] * 2,
        out_specs=pl.BlockSpec(memory_space=pltpu.VMEM),
        scratch_shapes=[
            pltpu.VMEM((NODES, NODES, elements), half),
            pltpu.VMEM((NODES, NODES, elements), half),
            pltpu.VMEM((128, FLAT), half),
            pltpu.VMEM((128, FLAT), half),
            pltpu.VMEM((FLAT, 128), half),
            pltpu.VMEM((FLAT, 128), half),
            dma((9,)),
            pltpu.VMEM((tiles, pairs * PACK_PITCH, 128), f32),
            pltpu.VMEM((tiles, pairs, 128, 128), half),
            pltpu.VMEM((tiles, pairs, 128, 128), half),
            pltpu.VMEM((tiles, pairs * ROW_PITCH, 128), f32),
            pltpu.VMEM((tiles, pairs * ROW_PITCH, 128), f32),
            pltpu.VMEM((tiles, pairs * ROW_PITCH, 128), f32),
            pltpu.VMEM((tiles, pairs * ROW_PITCH, 128), f32),
            pltpu.VMEM((tiles, pairs * ROW_PITCH, 128), f32),
            pltpu.VMEM((FLAT, TRACE), half),
            pltpu.VMEM((FLAT, FACES * SHORT), half),
            pltpu.VMEM((128, TRACE), half),
            pltpu.VMEM((128, TRACE), half),
            pltpu.VMEM((own, own), half),
            pltpu.VMEM((far, own), half),
            pltpu.VMEM((own, far), half),
            pltpu.VMEM((FLAT, elements), f32),
            pltpu.VMEM((FLAT, elements), f32),
            pltpu.VMEM((SIDE, own), f32),
            pltpu.VMEM((SIDE, own), half),
            pltpu.VMEM((SIDE, far), half),
            pltpu.VMEM((TRACE, elements), half),
            pltpu.VMEM((FACES * SHORT, elements), half),
            pltpu.VMEM((ROUNDS, SIDE, 128), f32),
            pltpu.VMEM((4, ROUNDS, SIDE, 128), f32),
            pltpu.VMEM((count, 8, 128), f32),
            pltpu.VMEM((count, 8, 128), f32),
            pltpu.VMEM((count, 8, 128), f32),
            pltpu.VMEM((count, 8, 128), f32),
            pltpu.VMEM((16, 16), f32),
            pltpu.VMEM((MODES * MODES, owned), f32),
            pltpu.VMEM((owned, MODES * 128), f32),
            pltpu.VMEM((128, elements), f32),
            dma((4, ROUNDS)),
            dma((4, ROUNDS)),
            dma,
            dma,
            dma,
            dma,
            pltpu.SemaphoreType.REGULAR((count.bit_length() - 1,)),
        ],
        compiler_params=pltpu.CompilerParams(
            collective_id=0, has_side_effects=True, vmem_limit_bytes=58 * 2**20
        ),
    )(
        rhs.T,
        elem_block.transpose(1, 2, 0),
        block_inv.transpose(1, 2, 0),
        flux_jac,
        face_src.T,
        send_face,
        elem_route.reshape(1, elements),
        agg_local.T,
        coarse_block.transpose(1, 2, 0),
        coarse_inv.transpose(1, 2, 0),
        *const_tables(),
    )
    return result.T


def solution(mesh):
    return jax.shard_map(
        local,
        mesh=mesh,
        in_specs=(
            P(("dom", "sub"), None),
            P(("dom", "sub"), None, None),
            P(("dom", "sub"), None, None),
            P(),
            P(("dom", "sub"), None),
            P(("dom", "sub"), None),
            P(("dom", "sub")),
            P(("dom", "sub"), None),
            P(("dom", "sub"), None, None),
            P(("dom", "sub"), None, None),
        ),
        out_specs=P(("dom", "sub"), None),
        check_vma=False,
    )
```

```python
import functools
import math

import jax
import jax.numpy as jnp
import numpy as np
from jax import lax
from jax.experimental import pallas as pl
from jax.experimental.pallas import tpu as pltpu
from jax.sharding import PartitionSpec as P

COMPS = 13
NODES = 64
FACES = 6
FACE_NODES = 16
MODES = 4
ROUNDS = 5
MOST = 2
FLAT = COMPS * NODES
ROW_PITCH = 40
PACK_PITCH = 136
SIDE = COMPS * FACE_NODES
TRACE = FACES * SIDE

SHORT = 48
PENALTY = 0.5
MESH = pl.DeviceIdType.MESH


def node_tables():
    points = np.array([-1.0, -1.0 / math.sqrt(5.0), 1.0 / math.sqrt(5.0), 1.0])
    weights = np.array([1.0, 5.0, 5.0, 1.0]) / 6.0
    grid_i, grid_j, grid_k = np.meshgrid(points, points, points, indexing="ij")
    weight_grid = weights[:, None, None] * weights[None, :, None] * weights[None, None, :] / 8.0
    basis = np.stack([np.ones(64), grid_i.reshape(-1), grid_j.reshape(-1), grid_k.reshape(-1)])
    restrict = basis * weight_grid.reshape(-1)[None, :]
    number = np.arange(64).reshape(4, 4, 4)
    sides = [number[0], number[3], number[:, 0], number[:, 3], number[:, :, 0], number[:, :, 3]]
    face_index = np.stack([side.reshape(-1) for side in sides])
    return basis, restrict, face_index


def const_tables():
    basis, restrict, face_index = node_tables()
    eye = np.eye(COMPS)
    comp_row = np.pad(np.tile(np.repeat(eye, FACE_NODES, axis=0), (FACES, 1)), ((0, 0), (0, 3))).T
    node = np.eye(NODES)[face_index]
    row_node = np.broadcast_to(node[:, None], (FACES, COMPS, FACE_NODES, NODES)).reshape(TRACE, NODES)
    select = np.kron(np.eye(2), node.reshape(FACES * FACE_NODES, NODES))
    restrict_t = np.zeros((128, FLAT))
    restrict_t[: COMPS * MODES] = np.kron(eye, restrict)
    basis_t = np.zeros((FLAT, 128))
    basis_t[:, : COMPS * MODES] = np.kron(eye, basis.T)
    to_short = np.zeros((FACES * SHORT, 128))
    from_short = np.zeros((TRACE, SHORT))
    normal = (1, 1, 2, 2, 3, 3)
    tangent = ((2, 3), (2, 3), (1, 3), (1, 3), (1, 2), (1, 2))
    for f in range(FACES):
        for c in range(COMPS):
            row = f * SHORT + 3 * c
            to_short[row, c * MODES] = 1.0
            to_short[row, c * MODES + normal[f]] = -1.0 if f % 2 == 0 else 1.0
            to_short[row + 1, c * MODES + tangent[f][0]] = 1.0
            to_short[row + 2, c * MODES + tangent[f][1]] = 1.0
            rows = slice(f * SIDE + c * FACE_NODES, f * SIDE + (c + 1) * FACE_NODES)
            from_short[rows, 3 * c] = 1.0
            from_short[rows, 3 * c + 1] = basis[tangent[f][0], face_index[f]]
            from_short[rows, 3 * c + 2] = basis[tangent[f][1], face_index[f]]
    pick = np.zeros((128, MODES * 128))
    coef = np.zeros((16, MODES * 128))
    for k in range(MODES):
        for c in range(COMPS):
            for m in range(MODES):
                pick[c * MODES + k, k * 128 + c * MODES + m] = 1.0
                coef[m * MODES + k, k * 128 + c * MODES + m] = 1.0
    half = jnp.bfloat16
    return (
        jnp.asarray(comp_row, half),
        jnp.asarray(row_node.T, half),
        jnp.asarray(select, half),
        jnp.asarray(to_short, half),
        jnp.asarray(from_short, half),
        *parts_of(restrict_t),
        *parts_of(basis_t),
        jnp.asarray(pick, half),
        jnp.asarray(coef, half),
    )


def parts_of(table):
    table = np.asarray(table, np.float32)
    high = table.astype(jnp.bfloat16)
    return jnp.asarray(high), jnp.asarray((table - high.astype(np.float32)).astype(jnp.bfloat16))


def dot(a, b):
    return jnp.dot(a, b, preferred_element_type=jnp.float32)


def general(a, b, dims):
    return lax.dot_general(a, b, (dims, ((), ())), preferred_element_type=jnp.float32)


def split(value):
    high = value.astype(jnp.bfloat16)
    return high, (value - high.astype(jnp.float32)).astype(jnp.bfloat16)


def dot_ones(ones, value, dims=((1,), (0,))):
    high, low = split(value)
    return general(ones, high, dims) + general(ones, low, dims)


def dot_split(value, ones, dims):
    high, low = split(value)
    return general(high, ones, dims) + general(low, ones, dims)


def dot_parts(table, value):
    high, low = split(value)
    return dot(table[0], high) + (dot(table[0], low) + dot(table[1], high))


def kernel(
    count, subs,
    rhs, blocks_far, inverse_far, jac, face_src, send_face, route, agg_local, cblock, cinv,
    comp_row, node_row, select, to_short, from_short,
    restrict_high_far, restrict_low_far, basis_high_far, basis_low_far, pick, coef,
    out,
    blocks, inverse, restrict_high, restrict_low, basis_high, basis_low, fetch_sem,
    stage, block_w, inverse_w, rhs_lam, state, work, resid_lam, delta,
    lift_t, lift_short, restrict_flux_high, restrict_flux_low, pick_local, pick_remote, pick_send,
    lifted, around, near, table, landed, jump, jump_short, sending, arriving,
    bucket, incoming, reply, answer, jac_pad, flat_solve, solve_wide, around_modes,
    send_sem, recv_sem, give_sem, take_sem, back_sem, home_sem, known,
):
    elements = rhs.shape[1]
    tiles = elements // 128
    own = FACES * elements
    far = ROUNDS * 128
    me = lax.axis_index("dom") * subs + lax.axis_index("sub")

    def place(flat):
        return (flat // subs, flat % subs)

    def partner(k):
        bit = 1 << k
        return me + bit * (1 - 2 * ((me // bit) % 2))

    slabs = [
        pltpu.make_async_copy(
            inverse_far.at[pl.ds(i * 16, 16)], inverse.at[pl.ds(i * 16, 16)], fetch_sem.at[5 + i]
        )
        for i in range(4)
    ]
    for slab in slabs:
        slab.start()
    fetches = [
        pltpu.make_async_copy(source, target, fetch_sem.at[i])
        for i, (source, target) in enumerate(
            (
                (blocks_far, blocks),
                (restrict_high_far, restrict_high),
                (restrict_low_far, restrict_low),
                (basis_high_far, basis_high),
                (basis_low_far, basis_low),
            )
        )
    ]
    barrier = pltpu.get_barrier_semaphore()

    bits = count.bit_length() - 1
    for k in range(bits):
        pl.semaphore_signal(barrier, inc=1, device_id=place(partner(k)), device_id_type=MESH)
    for fetch in fetches:
        fetch.start()

    half_lanes = lax.broadcasted_iota(jnp.int32, (32, 128), 1) < NODES
    pairs = elements // 8

    def pack(source, target, arrivals=()):
        def transpose(n, carry):
            rows = source[n].astype(jnp.float32)
            flat = jnp.concatenate([rows[:, :128], rows[:, 128:]], axis=0).T
            for y in range(2):
                even, odd = flat[y * 64 : y * 64 + 32], flat[y * 64 + 32 : y * 64 + 64]
                stage[y, pl.ds(n, pairs, stride=PACK_PITCH), :] = jnp.where(half_lanes, even, odd)
                stage[y, pl.ds(NODES + n, pairs, stride=PACK_PITCH), :] = jnp.where(half_lanes, odd, even)
            return carry

        for i in range(4):
            if arrivals:
                arrivals[i].wait()
            lax.fori_loop(i * 16, i * 16 + 16, transpose, 0, unroll=8)

        def cast(j, carry):
            rows = pl.ds(pl.multiple_of(j * PACK_PITCH, 8), 128)
            for y in range(2):
                target[y, j] = stage[y, rows, :].astype(jnp.bfloat16)
            return carry

        lax.fori_loop(0, pairs, cast, 0, unroll=4)

    lane = lax.broadcasted_iota(jnp.int32, (NODES, 128), 1)
    odd_lane = (lane // 32) % 2 == 1

    def to_lam(source, target):
        for c in range(COMPS):
            rows = slice(c * NODES, (c + 1) * NODES)
            low, high = source[rows, :128], source[rows, 128:]
            flat = jnp.concatenate(
                [jnp.where(odd_lane, high, low), jnp.where(odd_lane, low, high)], axis=0
            ).T
            for y in range(2):
                for x in range(2):
                    start = y * 64 + x * 32
                    target[y, pl.ds(16 * x + c, pairs, stride=ROW_PITCH), :] = flat[start : start + 32]

    def from_lam(source, emit):
        for c in range(COMPS):
            flat = jnp.concatenate(
                [
                    source[y, pl.ds(16 * x + c, pairs, stride=ROW_PITCH), :]
                    for y in range(2)
                    for x in range(2)
                ],
                axis=0,
            ).T
            even, odd = flat[:NODES], flat[NODES:]
            rows = slice(c * NODES, (c + 1) * NODES)
            emit(rows, slice(0, 128), jnp.where(odd_lane, odd, even))
            emit(rows, slice(128, 256), jnp.where(odd_lane, even, odd))

    low_half = half_lanes[:16]
    blank = jnp.zeros((16, 128), jnp.float32)

    def apply_blocks(load, weights, emit):
        def body(g, carry):
            for y in range(2):
                parts = []
                for i in range(2):
                    row = pl.multiple_of((2 * g + i) * ROW_PITCH, 8)
                    even = load(y, pl.ds(row, 16))
                    odd = pltpu.roll(load(y, pl.ds(row + 16, 16)), NODES, 1)
                    parts += [
                        jnp.where(low_half, even, blank),
                        jnp.where(low_half, odd, blank),
                        jnp.where(low_half, blank, even),
                        jnp.where(low_half, blank, odd),
                    ]
                left = jnp.concatenate(parts, axis=0).astype(jnp.bfloat16)
                right = weights[y, pl.ds(2 * g, 2)].reshape(256, 128)
                both = lax.dot_general(
                    left, right, (((1,), (1,)), ((), ())), preferred_element_type=jnp.float32
                )
                for i in range(2):
                    row = pl.multiple_of((2 * g + i) * ROW_PITCH, 8)
                    value = both[64 * i : 64 * i + 64, 128 * i : 128 * i + 128]
                    emit(y, pl.ds(row, 16), jnp.where(low_half, value[:16], value[32:48]))
                    emit(y, pl.ds(row + 16, 16), jnp.where(low_half, value[48:], value[16:32]))
            return carry

        lax.fori_loop(0, pairs // 2, body, 0, unroll=8)

    def load_from(source):
        return lambda y, rows: source[y, rows, :]

    def store(target):
        def emit(y, rows, value):
            target[y, rows, :] = value
        return emit

    def add_to(target):
        def emit(y, rows, value):
            target[y, rows, :] = target[y, rows, :] + value
        return emit

    def column(row):
        element = (row * 43691) >> 18
        return jnp.where(row < own, (row - element * FACES) * elements + element, row)

    def one_hot(rows, wanted, value=1.0):
        index = lax.broadcasted_iota(jnp.int32, (rows, wanted.shape[1]), 0)
        return jnp.where(index == wanted, value, 0.0).astype(jnp.bfloat16)

    for k in range(ROUNDS):
        wanted = column(send_face[k : k + 1, :])

        def send_rows(f, carry):
            rows = pl.ds(pl.multiple_of(f * elements, elements), elements)
            pick_send[rows, k * 128 : (k + 1) * 128] = one_hot(elements, wanted - f * elements)
            return carry

        lax.fori_loop(0, FACES, send_rows, 0)

    to_lam(rhs, rhs_lam)
    pack(inverse, inverse_w, slabs)
    apply_blocks(load_from(rhs_lam), inverse_w, store(state))

    def local_tables():
        jac_pad[...] = jnp.zeros_like(jac_pad)
        jac_pad[:COMPS, :COMPS] = PENALTY * jac[...]
        spread_jac = general(jac_pad[...].astype(jnp.bfloat16), comp_row[...], ((0,), (0,)))
        for c in range(COMPS):
            lift_t[c * NODES : (c + 1) * NODES, :] = node_row[...] * spread_jac[
                c : c + 1, :
            ].astype(jnp.bfloat16)
        row = lax.broadcasted_iota(jnp.int32, (elements, elements), 0)
        mine = jnp.where(row == lax.broadcasted_iota(jnp.int32, (elements, elements), 1), 1.0, 0.0)
        for f in range(FACES):
            lanes = slice(f * elements, (f + 1) * elements)
            wanted = column(face_src[f : f + 1, :])

            def local_rows(g, carry):
                rows = pl.ds(pl.multiple_of(g * elements, elements), elements)
                pick_local[rows, lanes] = one_hot(elements, wanted - g * elements, -1.0)
                return carry

            lax.fori_loop(0, FACES, local_rows, 0)
            pick_local[lanes, lanes] = pick_local[lanes, lanes] + mine.astype(jnp.bfloat16)

            def remote_rows(k, carry):
                rows = pl.ds(pl.multiple_of(k * 128, 128), 128)
                pick_remote[rows, lanes] = one_hot(128, wanted - own - k * 128, -1.0)
                return carry

            lax.fori_loop(0, ROUNDS, remote_rows, 0)

    odd_face = (lax.broadcasted_iota(jnp.int32, (FACES * FACE_NODES, 128), 1) // 32) % 2 == 1

    def traces():
        for c in range(COMPS):
            flat = jnp.concatenate(
                [
                    state[y, pl.ds(16 * x + c, pairs, stride=ROW_PITCH), :]
                    for y in range(2)
                    for x in range(2)
                ],
                axis=0,
            ).astype(jnp.bfloat16)
            value = general(select[...], flat, ((1,), (1,)))
            even, odd = value[: FACES * FACE_NODES], value[FACES * FACE_NODES :]
            low = jnp.where(odd_face, odd, even).astype(jnp.bfloat16)
            high = jnp.where(odd_face, even, odd).astype(jnp.bfloat16)
            rows = slice(c * FACE_NODES, (c + 1) * FACE_NODES)
            for f in range(FACES):
                part = slice(f * FACE_NODES, (f + 1) * FACE_NODES)
                table[rows, f * elements : f * elements + 128] = low[part]
                table[rows, f * elements + 128 : (f + 1) * elements] = high[part]

    def begin(number, rows):
        copies = {}
        for group in ((4,), (3,), (2, 1, 0)):
            lanes = slice(min(group) * 128, (max(group) + 1) * 128)
            outgoing = dot(table[:rows, :], pick_send[:, lanes])
            for k in group:
                start = (k - min(group)) * 128
                sending[k, :rows, :] = outgoing[:, start : start + 128]
                copies[k] = pltpu.make_async_remote_copy(
                    src_ref=sending.at[k, pl.ds(0, rows)],
                    dst_ref=arriving.at[number, k, pl.ds(0, rows)],
                    send_sem=send_sem.at[number, k],
                    recv_sem=recv_sem.at[number, k],
                    device_id=place(partner(k)),
                    device_id_type=MESH,
                )
                copies[k].start()
        return copies

    def end(number, rows, copies, target):
        def land(k):
            copies[k].wait_recv()
            landed[:rows, k * 128 : (k + 1) * 128] = arriving[number, k, :rows, :].astype(
                jnp.bfloat16
            )

        for k in (0, 1, 2):
            land(k)
        near[:rows, :] = near[:rows, :] + dot(landed[:rows, : 3 * 128], pick_remote[: 3 * 128, :])
        for k in (3, 4):
            land(k)
        value = near[:rows, :] + dot(landed[:rows, 3 * 128 :], pick_remote[3 * 128 :, :])
        for f in range(FACES):
            target[f * rows : (f + 1) * rows, :] = value[:, f * elements : (f + 1) * elements].astype(
                jnp.bfloat16
            )
        for k in range(ROUNDS):
            copies[k].wait_send()

    def operate(number, between=None, beside=None):
        traces()
        copies = begin(number, SIDE)
        if between is not None:
            between()
        near[...] = dot(table[...], pick_local[...])
        apply_blocks(load_from(state), block_w, store(work))
        if beside is not None:
            beside()
        end(number, SIDE, copies, jump)

    def residual(y, rows):
        return rhs_lam[y, rows, :] - work[y, rows, :] - delta[y, rows, :]

    def sweep(number, between=None):
        operate(number, between)
        lifted[...] = dot(lift_t[...], jump[...])
        to_lam(lifted, delta)
        apply_blocks(residual, inverse_w, add_to(state))

    def exchange(source, target, sent, got, between=None):
        def copy_of(step):
            other = (me + step) % count
            return pltpu.make_async_remote_copy(
                src_ref=source.at[other, pl.ds(0, MOST)],
                dst_ref=target.at[me, pl.ds(0, MOST)],
                send_sem=sent,
                recv_sem=got,
                device_id=place(other),
                device_id_type=MESH,
            )

        def start(step, carry):
            copy_of(step).start()
            return carry

        lax.fori_loop(1, count, start, 0, unroll=4)
        target[me] = source[me]
        if between is not None:
            between()
        everything = pl.ds(0, count - 1), pl.ds(0, MOST)
        for semaphore in (got, sent):
            pltpu.make_async_copy(source.at[everything], target.at[everything], semaphore).wait()

    told = []

    def tell():
        if told:
            pl.semaphore_wait(known.at[told[-1]], 1)
        if len(told) < bits:
            k = len(told)
            pl.semaphore_signal(
                known.at[k], inc=1, device_id=place(partner(k)), device_id_type=MESH
            )
            told.append(k)

    def behind_first():
        tell()
        local_tables()
        tell()
        for fetch in fetches:
            fetch.wait()
        pack(blocks, block_w)
        tell()

    owned = cblock.shape[2]
    inverse_rows = [cinv[m] for m in range(MODES)]
    block_rows = [cblock[m] for m in range(MODES)]

    def times(rows, k, other):
        return rows[k : k + 1, :] * other

    def solve_rows():
        inner = [
            sum(times(block_rows[p], q, inverse_rows[q]) for q in range(MODES)) for p in range(MODES)
        ]
        for m in range(MODES):
            flat_solve[m * MODES : (m + 1) * MODES, :] = 2.0 * inverse_rows[m] - sum(
                times(inverse_rows[m], p, inner[p]) for p in range(MODES)
            )

    solve_rows()
    pl.semaphore_wait(barrier, bits)
    sweep(0, behind_first)

    held = []

    def behind_second():
        tell()
        route_row = (route[...] // MOST) * 8 + route[...] % MOST
        held.append(one_hot(count * 8, route_row))
        held.extend(one_hot(owned, agg_local[s : s + 1, :]) for s in range(MOST))
        reply[...] = jnp.zeros_like(reply)

        def emit_around(rows, lanes, value):
            around[rows, lanes] = rhs[rows, lanes] - value

        from_lam(work, emit_around)
        around_modes[...] = dot_parts((restrict_high[...], restrict_low[...]), around[...])
        for f in range(FACES):
            rows = slice(f * SIDE, (f + 1) * SIDE)
            lift_short[:, f * SHORT : (f + 1) * SHORT] = dot(
                lift_t[:, rows], from_short[rows, :]
            ).astype(jnp.bfloat16)
        high, low = split(
            dot(restrict_high[...], lift_t[...]) + dot(restrict_low[...], lift_t[...])
        )
        restrict_flux_high[...] = high
        restrict_flux_low[...] = low
        solve_wide[...] = dot_split(flat_solve[...], coef[...], ((0,), (0,)))

    operate(1, between=tell, beside=behind_second)
    while len(told) < bits:
        tell()
    tell()
    partial = around_modes[...] - (
        dot(restrict_flux_high[...], jump[...]) + dot(restrict_flux_low[...], jump[...])
    )
    to_bucket = held[0]
    bucket[...] = dot_ones(to_bucket, partial, ((1,), (1,))).reshape(count, 8, 128)

    def behind_bucket():
        lifted[...] = dot(lift_t[...], jump[...])
        to_lam(lifted, delta)
        resid_lam[...] = rhs_lam[...] - work[...] - delta[...]

    exchange(bucket, incoming, give_sem, take_sem, behind_bucket)
    members = held[1:]
    coarse_rhs = sum(dot_ones(members[s], incoming[:, s, :]) for s in range(MOST))
    product = solve_wide[...] * dot_split(coarse_rhs, pick[...], ((1,), (0,)))
    solved = product[:, :128] + product[:, 128:256] + product[:, 256:384] + product[:, 384:]
    for s in range(MOST):
        reply[:, s, :] = dot_ones(members[s], solved, ((0,), (0,)))
    exchange(reply, answer, back_sem, home_sem)
    slot = lax.broadcasted_iota(jnp.int32, (count * 8, 128), 0) % 8
    returned = jnp.where(slot < MOST, answer[...].reshape(count * 8, 128), 0.0)
    correction = dot_split(returned, to_bucket, ((0,), (0,)))

    short = dot_ones(to_short[...], correction).astype(jnp.bfloat16)
    for f in range(FACES):
        table[:SHORT, f * elements : (f + 1) * elements] = short[f * SHORT : (f + 1) * SHORT]
    copies = begin(2, SHORT)
    lifted[...] = dot_parts((basis_high[...], basis_low[...]), correction)
    to_lam(lifted, delta)
    state[...] = state[...] + delta[...]

    def take_from_residual(y, rows, value):
        resid_lam[y, rows, :] = resid_lam[y, rows, :] - value

    apply_blocks(load_from(delta), block_w, take_from_residual)
    near[:SHORT, :] = dot(table[:SHORT, :], pick_local[...])
    end(2, SHORT, copies, jump_short)
    lifted[...] = dot(lift_short[...], jump_short[...])
    to_lam(lifted, delta)

    def coarse_residual(y, rows):
        return resid_lam[y, rows, :] - delta[y, rows, :]

    apply_blocks(coarse_residual, inverse_w, add_to(state))
    sweep(3)

    def emit_out(rows, lanes, value):
        out[rows, lanes] = value

    from_lam(state, emit_out)


def local(
    rhs,
    elem_block,
    block_inv,
    flux_jac,
    face_src,
    send_face,
    elem_route,
    agg_local,
    coarse_block,
    coarse_inv,
):
    elements = rhs.shape[0]
    count = lax.axis_size(("dom", "sub"))
    subs = lax.axis_size("sub")
    owned = coarse_block.shape[0]
    tiles = elements // 128
    pairs = elements // 8
    own = FACES * elements
    far = ROUNDS * 128
    f32, half = jnp.float32, jnp.bfloat16
    dma = pltpu.SemaphoreType.DMA
    near_spec = pl.BlockSpec(memory_space=pltpu.VMEM)
    far_spec = pl.BlockSpec(memory_space=pl.ANY)
    result = pl.pallas_call(
        functools.partial(kernel, count, subs),
        out_shape=jax.ShapeDtypeStruct((FLAT, elements), f32),
        in_specs=[near_spec, far_spec, far_spec] + [near_spec] * 12 + [far_spec] * 4 + [near_spec] * 2,
        out_specs=pl.BlockSpec(memory_space=pltpu.VMEM),
        scratch_shapes=[
            pltpu.VMEM((NODES, NODES, elements), half),
            pltpu.VMEM((NODES, NODES, elements), half),
            pltpu.VMEM((128, FLAT), half),
            pltpu.VMEM((128, FLAT), half),
            pltpu.VMEM((FLAT, 128), half),
            pltpu.VMEM((FLAT, 128), half),
            dma((9,)),
            pltpu.VMEM((tiles, pairs * PACK_PITCH, 128), f32),
            pltpu.VMEM((tiles, pairs, 128, 128), half),
            pltpu.VMEM((tiles, pairs, 128, 128), half),
            pltpu.VMEM((tiles, pairs * ROW_PITCH, 128), f32),
            pltpu.VMEM((tiles, pairs * ROW_PITCH, 128), f32),
            pltpu.VMEM((tiles, pairs * ROW_PITCH, 128), f32),
            pltpu.VMEM((tiles, pairs * ROW_PITCH, 128), f32),
            pltpu.VMEM((tiles, pairs * ROW_PITCH, 128), f32),
            pltpu.VMEM((FLAT, TRACE), half),
            pltpu.VMEM((FLAT, FACES * SHORT), half),
            pltpu.VMEM((128, TRACE), half),
            pltpu.VMEM((128, TRACE), half),
            pltpu.VMEM((own, own), half),
            pltpu.VMEM((far, own), half),
            pltpu.VMEM((own, far), half),
            pltpu.VMEM((FLAT, elements), f32),
            pltpu.VMEM((FLAT, elements), f32),
            pltpu.VMEM((SIDE, own), f32),
            pltpu.VMEM((SIDE, own), half),
            pltpu.VMEM((SIDE, far), half),
            pltpu.VMEM((TRACE, elements), half),
            pltpu.VMEM((FACES * SHORT, elements), half),
            pltpu.VMEM((ROUNDS, SIDE, 128), f32),
            pltpu.VMEM((4, ROUNDS, SIDE, 128), f32),
            pltpu.VMEM((count, 8, 128), f32),
            pltpu.VMEM((count, 8, 128), f32),
            pltpu.VMEM((count, 8, 128), f32),
            pltpu.VMEM((count, 8, 128), f32),
            pltpu.VMEM((16, 16), f32),
            pltpu.VMEM((MODES * MODES, owned), f32),
            pltpu.VMEM((owned, MODES * 128), f32),
            pltpu.VMEM((128, elements), f32),
            dma((4, ROUNDS)),
            dma((4, ROUNDS)),
            dma,
            dma,
            dma,
            dma,
            pltpu.SemaphoreType.REGULAR((count.bit_length() - 1,)),
        ],
        compiler_params=pltpu.CompilerParams(
            collective_id=0, has_side_effects=True, vmem_limit_bytes=58 * 2**20
        ),
    )(
        rhs.T,
        elem_block.transpose(1, 2, 0),
        block_inv.transpose(1, 2, 0),
        flux_jac,
        face_src.T,
        send_face,
        elem_route.reshape(1, elements),
        agg_local.T,
        coarse_block.transpose(1, 2, 0),
        coarse_inv.transpose(1, 2, 0),
        *const_tables(),
    )
    return result.T


def solution(mesh):
    return jax.shard_map(
        local,
        mesh=mesh,
        in_specs=(
            P(("dom", "sub"), None),
            P(("dom", "sub"), None, None),
            P(("dom", "sub"), None, None),
            P(),
            P(("dom", "sub"), None),
            P(("dom", "sub"), None),
            P(("dom", "sub")),
            P(("dom", "sub"), None),
            P(("dom", "sub"), None, None),
            P(("dom", "sub"), None, None),
        ),
        out_specs=P(("dom", "sub"), None),
        check_vma=False,
    )
```
